128 devices in a mesh: ctx: 32 (over y, z, core), exp: 4 (over x).
Axes of the slice: x: 4, y: 4, z: 4, core: 2. Of those that a mesh axis runs over, the one named last changes fastest.
Arguments:
- queries: bfloat16 [16384, 4096], P('ctx', 'exp'), may hold values from -6 to 6
- key_vectors: bfloat16 [16384, 4096], P('ctx', 'exp'), may hold values from -6 to 6
- value_vectors: bfloat16 [16384, 4096], P('ctx', 'exp'), may hold values from -6 to 6
- spikes: int32 [16384, 32], P('ctx', 'exp'), may hold values 0 or 1
- routes: int32 [16384, 2], P(('ctx', 'exp')), may hold values from 0 to 63, all different within a row; in each aligned block of 128 rows (0 to 127, 128 to 255, ...) at most 6 rows name the same one
- route_probs: bfloat16 [16384, 2], P(('ctx', 'exp')), may hold values from 0.099609375 to 1
- gate_weight: bfloat16 [128, 4096, 384], P(('ctx', 'exp')), may hold values from -0.09375 to 0.09375
- up_weight: bfloat16 [128, 4096, 384], P(('ctx', 'exp')), may hold values from -0.09375 to 0.09375
- down_weight: bfloat16 [128, 384, 4096], P(('ctx', 'exp')), may hold values from -0.21875 to 0.21875
- out_grad: bfloat16 [16384, 4096], P(('ctx', 'exp')), may hold values from -6 to 6
Outputs:
- grad_queries: bfloat16 [16384, 4096], P('ctx', 'exp')
- grad_keys: bfloat16 [16384, 4096], P('ctx', 'exp')
- grad_values: bfloat16 [16384, 4096], P('ctx', 'exp')
- grad_gate: bfloat16 [128, 4096, 384], P(('ctx', 'exp'))
- grad_up: bfloat16 [128, 4096, 384], P(('ctx', 'exp'))
- grad_down: bfloat16 [128, 384, 4096], P(('ctx', 'exp'))
The draws below stay inside these ranges and needn't reach their ends.
Inputs may be any that keep to these rules, and one draw needn't show every extreme that they name: The 2 experts of a token differ. Among the routes of one route block of 128 positions no expert is named more than 6 times, and in some blocks one expert is named exactly 6 times.
All inputs are finite; a program needn't handle non-finite values. No bound on the sum of `spikes` on one device may be relied on, other than what follows from the above.
Results may differ from the reference program's by a relative error of at most 0.015.
Values may be sent and summed in bfloat16 or wider, within the bound.
No kernel may reach another device: no remote copies, remote signals or barrier semaphores. Data moves between devices by JAX's collectives and lax.ppermute only.
A program may use at most 192 MiB of HBM per device.

```python
import math
import jax
import jax.numpy as jnp
import numpy as np
from jax import lax

HD = 128
HEADS = 32
D = 4096
FF = 768
TOPK = 2
S_DEV = 512
TOK = 128
LEN = 16384
EXPERTS = 64
HALVES = 128
FFH = 384
CAP = 6
N_CTX = 32
N_EXP = 4


def touch_ends(result, own_key, low, largest):
    extent = result.shape
    spot = [jax.random.randint(jax.random.fold_in(own_key, axis), (), 0, extent[axis]) for axis in range(len(extent))]
    result = result.at[tuple(spot)].set(low)
    longest = extent.index(max(extent))
    spot[longest] = (spot[longest] + 1) % extent[longest]
    return result.at[tuple(spot)].set(largest)


def shard_levels(rng, dims, split, smallest, largest):
    loudness = 1.0
    for position, shards_of in split:
        heights = jax.random.uniform(jax.random.fold_in(jax.random.fold_in(rng, 6), position), (shards_of,), jnp.float32, smallest / len(split), largest / len(split))
        loudness = loudness * jnp.repeat(jnp.exp(heights), dims[position] // shards_of).reshape((-1,) + (1,) * (len(dims) - 1 - position))
    return loudness


def shared_out(rng, own, number, rows, number_of, top, reach, lean):
    sequence = jax.random.permutation(rng, number_of)
    crowded, ordinary = load_shares(number_of, rows * top, reach, lean, True), load_shares(number_of, rows * top, reach, lean, False)
    places = jnp.arange(number_of)

    def named(lengths, offset_by):
        used = int((lengths > 0).sum())
        fixed = max(1, used // 4)
        moved = fixed + (places - fixed + offset_by * (used - fixed)) % max(1, number_of - fixed)
        return jnp.zeros((number_of,), jnp.int32).at[sequence[jnp.where(places < fixed, places, moved)]].set(jnp.asarray(lengths, jnp.int32))

    lengths = jnp.where(number % 4 == 0, named(crowded, number // 4), named(ordinary, number - number // 4 - 1))
    mixed = jax.random.permutation(jax.random.fold_in(own, 3), number_of)
    source_of, receiver = mixed[0:number_of // 2 * 2:2], mixed[1:number_of // 2 * 2:2]
    margin = jnp.minimum(lengths[source_of] - 1, reach - lengths[receiver]) // 2
    margin = jnp.where((source_of == sequence[0]) | (receiver == sequence[0]) | (lengths[receiver] == 0), 0, jnp.maximum(margin, 0))
    moved = jax.random.randint(jax.random.fold_in(own, 4), (number_of // 2,), 0, 1 << 20) % (margin + 1)
    lengths = lengths.at[source_of].add(-moved).at[receiver].add(moved)
    items = jnp.searchsorted(jnp.cumsum(lengths), jnp.arange(rows * top), side="right").astype(jnp.int32)
    listing = items.reshape(top, rows).T
    listing = listing[jax.random.permutation(jax.random.fold_in(own, 1), rows)]
    offset_by = jax.random.randint(jax.random.fold_in(own, 2), (rows, 1), 0, top)
    return jnp.take_along_axis(listing, (jnp.arange(top)[None, :] + offset_by) % top, axis=1)


def load_shares(count, total, limit, lean, full):
    portions = [(1 << 20) // math.isqrt(standing ** lean) + 1 for standing in range(1, count + 1)]
    largest = limit if full else min(limit, max(-(-total // count), total * portions[0] // sum(portions)))
    least = 1 if total - largest >= count - 1 else 0
    holding, surplus = [largest] + [least] * (count - 1), total - largest - least * (count - 1)
    while surplus > 0:
        free = [i for i in range(1, count) if holding[i] < largest] or [i for i in range(1, count) if holding[i] < limit]
        mass, budget = sum([portions[i] for i in free]), surplus
        for i in free:
            extra = min(limit - holding[i], max(1, budget * portions[i] // mass), surplus)
            holding[i] = holding[i] + extra
            surplus = surplus - extra
    return np.array(holding)


def noise(own_key, extent, spread, bound, cuts=(), kind=jnp.bfloat16):
    gain = shard_levels(own_key, extent, cuts, -0.22, 0.18) if cuts else 1.0
    drawn = jax.random.normal(own_key, extent, jnp.float32) * spread * gain
    return jnp.minimum(jnp.maximum(drawn, -bound), bound).astype(kind)


def setup_inputs(seed: int = 0) -> dict:
    key_list = jax.random.split(jax.random.key(seed), 11)
    queries = noise(key_list[0], (LEN, D), 1.0, 6.0, ((0, 32), (1, 4)))
    key_vectors = noise(key_list[1], (LEN, D), 1.0, 6.0, ((0, 32), (1, 4)))
    value_vectors = noise(key_list[2], (LEN, D), 1.0, 6.0, ((0, 32), (1, 4)))
    spikes = touch_ends((jax.random.randint(key_list[3], (LEN, HEADS), 0, 2) < 1).astype(jnp.int32), jax.random.fold_in(key_list[3], 1), 0, 1)
    routes_keys = jax.random.split(jax.random.fold_in(key_list[4], 1), LEN // TOK)
    routes_turns = jax.random.permutation(jax.random.fold_in(key_list[4], 3), LEN // TOK)
    routes = jax.vmap(lambda own, number: shared_out(jax.random.fold_in(key_list[4], 2), own, number, TOK, EXPERTS, TOPK, CAP, 2))(routes_keys, routes_turns).reshape((LEN, TOPK))
    route_probs = jnp.clip(0.099609375 + 0.9003906 * jax.random.uniform(key_list[5], (LEN, TOPK), jnp.float32) ** shard_levels(key_list[5], (LEN, TOPK), ((0, 128),), -0.2, 0.2), 0.099609375, 1.0).astype(jnp.bfloat16)
    gate_weight = noise(key_list[6], (HALVES, D, FFH), D ** -0.5, 0.09375, ((0, 128),))
    up_weight = noise(key_list[7], (HALVES, D, FFH), D ** -0.5, 0.09375, ((0, 128),))
    down_weight = noise(key_list[8], (HALVES, FFH, D), FF ** -0.5, 0.21875, ((0, 128),))
    out_grad = noise(key_list[9], (LEN, D), 0.5, 6.0, ((0, 128),))
    return dict(queries=queries, key_vectors=key_vectors, value_vectors=value_vectors, spikes=spikes, routes=routes, route_probs=route_probs, gate_weight=gate_weight, up_weight=up_weight, down_weight=down_weight, out_grad=out_grad)


def causal_scores(left_side, right_side, causal):
    product = jnp.einsum('bti,bsi->bts', left_side.astype(jnp.float32), right_side.astype(jnp.float32), precision=lax.Precision.HIGHEST)
    return jnp.where(causal, product, 0.0).astype(jnp.bfloat16)

def forward_head(packed):
    query, masked, value_block = packed
    scaling = 1.0 / math.sqrt(HD * LEN)
    positions = jnp.arange(S_DEV)
    causal = (positions[:, None] >= positions[None, :])[None]
    block_states = jnp.einsum('bsi,bsj->bij', masked.astype(jnp.float32), value_block.astype(jnp.float32), precision=lax.Precision.HIGHEST)
    shifted = jnp.concatenate([jnp.zeros_like(block_states[:1]), block_states[:-1]], axis=0)
    states_in = jnp.cumsum(shifted, axis=0)
    scores = causal_scores(query, masked, causal)
    intra = jnp.einsum('bts,bsd->btd', scores.astype(jnp.float32), value_block.astype(jnp.float32), precision=lax.Precision.HIGHEST)
    inter = jnp.einsum('bti,bij->btj', query.astype(jnp.float32), states_in, precision=lax.Precision.HIGHEST)
    attended = (scaling * (intra + inter)).astype(jnp.bfloat16)
    return (attended, states_in)

def backward_head(packed):
    query, masked, value_block, spike_block, states_in, attended_grad = packed
    scaling = 1.0 / math.sqrt(HD * LEN)
    positions = jnp.arange(S_DEV)
    causal = (positions[:, None] >= positions[None, :])[None]
    scores = causal_scores(query, masked, causal)
    grad_f = attended_grad.astype(jnp.float32)
    local_grad = scaling * jnp.einsum('bti,btj->bij', query.astype(jnp.float32), grad_f, precision=lax.Precision.HIGHEST)
    inclusive = jnp.cumsum(local_grad[::-1], axis=0)[::-1]
    grad_states = jnp.concatenate([inclusive[1:], jnp.zeros_like(inclusive[:1])], axis=0)
    back_scores = causal_scores(attended_grad, value_block, causal).astype(jnp.float32)
    grad_query = scaling * (jnp.einsum('bts,bsd->btd', back_scores, masked.astype(jnp.float32), precision=lax.Precision.HIGHEST) + jnp.einsum('btj,bij->bti', grad_f, states_in, precision=lax.Precision.HIGHEST))
    grad_key = spike_block[..., None] * (scaling * jnp.einsum('bts,btd->bsd', back_scores, query.astype(jnp.float32), precision=lax.Precision.HIGHEST) + jnp.einsum('bsj,bij->bsi', value_block.astype(jnp.float32), grad_states, precision=lax.Precision.HIGHEST))
    grad_value = scaling * jnp.einsum('bts,btd->bsd', scores.astype(jnp.float32), grad_f, precision=lax.Precision.HIGHEST) + jnp.einsum('bsi,bij->bsj', masked.astype(jnp.float32), grad_states, precision=lax.Precision.HIGHEST)
    return (grad_query.astype(jnp.bfloat16), grad_key.astype(jnp.bfloat16), grad_value.astype(jnp.bfloat16))

def reference(queries, key_vectors, value_vectors, spikes, routes, route_probs, gate_weight, up_weight, down_weight, out_grad):
    device_total = N_CTX * N_EXP

    def heads_view(array):
        return array.reshape(N_CTX, S_DEV, HEADS, HD).transpose(2, 0, 1, 3)

    def heads_back(array):
        return array.transpose(1, 2, 0, 3).reshape(LEN, D)
    spike_f = spikes.astype(jnp.float32)
    masked_flat = (key_vectors.reshape(LEN, HEADS, HD).astype(jnp.float32) * spike_f[:, :, None]).astype(jnp.bfloat16).reshape(LEN, D)
    query_all = heads_view(queries)
    masked_all = heads_view(masked_flat)
    value_all = heads_view(value_vectors)
    spike_all = spike_f.reshape(N_CTX, S_DEV, HEADS).transpose(2, 0, 1)
    attended, states_in = lax.map(forward_head, (query_all, masked_all, value_all))
    rows_flat = heads_back(attended)
    block_routes = routes.reshape(device_total, TOK * TOPK)
    onehot = (block_routes[:, :, None] == jnp.arange(EXPERTS, dtype=jnp.int32)[None, None, :]).astype(jnp.int32)
    earlier = jnp.cumsum(onehot, axis=1) - onehot
    slot_index = lax.optimization_barrier(jnp.sum(earlier * onehot, axis=2)).astype(jnp.int32)
    block_ids = jnp.arange(device_total, dtype=jnp.int32)
    device_grid = jnp.broadcast_to(block_ids[:, None], block_routes.shape)
    token_ids = (block_ids[:, None] * TOK + jnp.arange(TOK * TOPK, dtype=jnp.int32)[None, :] // TOPK).astype(jnp.int32)
    table = jnp.full((EXPERTS, device_total, CAP), LEN, jnp.int32)
    table = table.at[block_routes, device_grid, slot_index].set(token_ids)
    prob_table = jnp.zeros((EXPERTS, device_total, CAP), jnp.float32)
    prob_table = prob_table.at[block_routes, device_grid, slot_index].set(route_probs.reshape(device_total, TOK * TOPK).astype(jnp.float32))
    padded_rows = jnp.concatenate([rows_flat, jnp.zeros((1, D), jnp.bfloat16)], axis=0)
    padded_grad = jnp.concatenate([out_grad, jnp.zeros((1, D), jnp.bfloat16)], axis=0)
    gate_pairs = gate_weight.reshape(EXPERTS, 2, D, FFH)
    up_pairs = up_weight.reshape(EXPERTS, 2, D, FFH)
    down_pairs = down_weight.reshape(EXPERTS, 2, FFH, D)

    def expert_step(moe_grad, packed):
        index_table, prob_rows, gate_pair, up_pair, down_pair = packed
        index_flat = index_table.reshape(-1)
        expert_rows = padded_rows[index_flat]
        grad_rows = (padded_grad[index_flat].astype(jnp.float32) * prob_rows.reshape(-1)[:, None]).astype(jnp.bfloat16)
        row_total = jnp.zeros((index_flat.shape[0], D), jnp.float32)
        gate_grads = []
        up_grads = []
        down_grads = []
        for half_id in range(2):
            gate_value = jnp.dot(expert_rows, gate_pair[half_id], preferred_element_type=jnp.float32)
            up_value = jnp.dot(expert_rows, up_pair[half_id], preferred_element_type=jnp.float32)
            sigmoid_gate = jax.nn.sigmoid(gate_value)
            silu_gate = gate_value * sigmoid_gate
            hidden = (silu_gate * up_value).astype(jnp.bfloat16)
            down_grads.append(jnp.dot(hidden.T, grad_rows, preferred_element_type=jnp.float32).astype(jnp.bfloat16))
            hidden_grad = jnp.dot(grad_rows, down_pair[half_id].T, preferred_element_type=jnp.float32)
            gate_grad = (hidden_grad * up_value * (sigmoid_gate * (1.0 + gate_value * (1.0 - sigmoid_gate)))).astype(jnp.bfloat16)
            up_grad = (hidden_grad * silu_gate).astype(jnp.bfloat16)
            gate_grads.append(jnp.dot(expert_rows.T, gate_grad, preferred_element_type=jnp.float32).astype(jnp.bfloat16))
            up_grads.append(jnp.dot(expert_rows.T, up_grad, preferred_element_type=jnp.float32).astype(jnp.bfloat16))
            row_part = jnp.dot(gate_grad, gate_pair[half_id].T, preferred_element_type=jnp.float32) + jnp.dot(up_grad, up_pair[half_id].T, preferred_element_type=jnp.float32)
            row_total = row_total + row_part
        row_grads = row_total.astype(jnp.bfloat16)
        moe_grad = moe_grad.at[index_flat].add(row_grads.astype(jnp.float32))
        return (moe_grad, (jnp.stack(gate_grads), jnp.stack(up_grads), jnp.stack(down_grads)))
    moe_grad, stacked = lax.scan(expert_step, jnp.zeros((LEN + 1, D), jnp.float32), (table, prob_table, gate_pairs, up_pairs, down_pairs))
    grad_gate = stacked[0].reshape(HALVES, D, FFH)
    grad_up = stacked[1].reshape(HALVES, D, FFH)
    grad_down = stacked[2].reshape(HALVES, FFH, D)
    attended_grad = (out_grad.astype(jnp.float32) + moe_grad[:LEN]).astype(jnp.bfloat16)
    grad_heads = heads_view(attended_grad)
    grad_query, grad_key, grad_value = lax.map(backward_head, (query_all, masked_all, value_all, spike_all, states_in, grad_heads))
    return (heads_back(grad_query), heads_back(grad_key), heads_back(grad_value), grad_gate, grad_up, grad_down)
```

```python
import functools
import math

import jax
import jax.numpy as jnp
from jax import lax
from jax.experimental import pallas as pl
from jax.experimental.pallas import tpu as pltpu
from jax.sharding import PartitionSpec as P

F32 = jnp.float32
BF16 = jnp.bfloat16
NN = (((1,), (0,)), ((), ()))
NT = (((1,), (1,)), ((), ()))
TN = (((0,), (0,)), ((), ()))


def mm(a, b, dims=NN):
    return lax.dot_general(a, b, dims, preferred_element_type=F32)


def call(body, grid, in_specs, out_specs, out_shape, flops, nbytes, vmem=32, **kw):
    return pl.pallas_call(
        body,
        grid=grid,
        in_specs=in_specs,
        out_specs=out_specs,
        out_shape=out_shape,
        compiler_params=pltpu.CompilerParams(
            dimension_semantics=("arbitrary",) * len(grid), vmem_limit_bytes=vmem << 20
        ),
        cost_estimate=pl.CostEstimate(
            flops=int(flops), bytes_accessed=int(nbytes), transcendentals=0
        ),
        **kw,
    )


def spike_columns(spikes, pair, width, head):
    heads = spikes.shape[1]
    col = lax.broadcasted_iota(jnp.int32, (heads, width), 1) // head + pair * (width // head)
    row = lax.broadcasted_iota(jnp.int32, (heads, width), 0)
    spread = jnp.where(col == row, 1.0, 0.0).astype(BF16)
    return mm(spikes.astype(F32).astype(BF16), spread)


def state_body(head, k_ref, v_ref, s_ref, bs_ref, mk_ref):
    width = k_ref.shape[1]
    gate = spike_columns(s_ref[...], pl.program_id(0), width, head)
    masked = (k_ref[...].astype(F32) * gate).astype(BF16)
    mk_ref[...] = masked
    value = v_ref[...]
    for h in range(width // head):
        cols = slice(h * head, (h + 1) * head)
        bs_ref[cols, :] = mm(masked[:, cols], value[:, cols], TN).astype(BF16)


def intra_body(head, q_ref, mk_ref, v_ref, o_ref):
    length, width = q_ref.shape
    t = lax.broadcasted_iota(jnp.int32, (length, length), 0)
    s = lax.broadcasted_iota(jnp.int32, (length, length), 1)
    for h in range(width // head):
        cols = slice(h * head, (h + 1) * head)
        scores = mm(q_ref[:, cols], mk_ref[:, cols], NT)
        scores = jnp.where(t >= s, scores, 0.0).astype(BF16)
        o_ref[:, cols] = mm(scores, v_ref[:, cols])


def sum_body(reverse, x_ref, o_ref):
    count = x_ref.shape[0]

    def step(i, total):
        at = count - 1 - i if reverse else i
        o_ref[at] = total.astype(BF16)
        return total + x_ref[at].astype(F32)

    lax.fori_loop(0, count, step, jnp.zeros(x_ref.shape[1:], F32))


def select_body(pack_ref, m_ref, w_ref, mt_ref):
    rows, tokens = m_ref.shape
    pack = pack_ref[0]
    first, second = pack[0:1, :], pack[1:2, :]
    place = lax.broadcasted_iota(jnp.int32, (rows, tokens), 0).astype(F32)
    hit0, hit1 = place == first, place == second
    m_ref[...] = jnp.where(hit0 | hit1, 1.0, 0.0).astype(BF16)
    w_ref[...] = jnp.where(hit0, pack[2:3, :], jnp.where(hit1, pack[3:4, :], 0.0)).astype(BF16)
    eye = lax.broadcasted_iota(jnp.int32, (tokens, tokens), 0) == lax.broadcasted_iota(
        jnp.int32, (tokens, tokens), 1
    )
    first = jnp.sum(jnp.where(eye, first, 0.0), axis=1, keepdims=True)
    second = jnp.sum(jnp.where(eye, second, 0.0), axis=1, keepdims=True)
    place = lax.broadcasted_iota(jnp.int32, (tokens, rows), 1).astype(F32)
    mt_ref[...] = jnp.where((place == first) | (place == second), 1.0, 0.0).astype(BF16)


def put_rows(m_ref, columns, o_ref):
    rows = o_ref.shape[2]
    for p in range(2):
        picked = mm(m_ref[p * rows : (p + 1) * rows, :], columns).astype(BF16)
        o_ref[p, 0] = picked
        o_ref[p, 1] = picked


def grads_body(w_ref, g_ref, o_ref):
    put_rows(w_ref, g_ref[...], o_ref)


def rows_body(head, scaling, m_ref, q_ref, intra_ref, s_ref, buf_ref, o_ref):
    del buf_ref
    width = q_ref.shape[1]
    parts = []
    for h in range(width // head):
        cols = slice(h * head, (h + 1) * head)
        inter = mm(q_ref[:, cols], s_ref[cols, :])
        parts.append((scaling * (intra_ref[:, cols] + inter)).astype(BF16))
    put_rows(m_ref, jnp.concatenate(parts, axis=1), o_ref)


def expert_body(
    steps, chunk, r_ref, g_ref, wg_ref, wu_ref, wd_ref,
    ret_ref, h_ref, gg_ref, ug_ref, gate, up, hid,
):
    i = pl.program_id(0)
    count = r_ref.shape[0] // chunk

    @pl.when(i == 0)
    def _():
        gate[...] = jnp.zeros_like(gate)
        up[...] = jnp.zeros_like(up)
        hid[...] = jnp.zeros_like(hid)

    @pl.when(i < steps)
    def _():
        @pl.loop(0, count)
        def _(c):
            rows = pl.ds(pl.multiple_of(c * chunk, chunk), chunk)
            x = r_ref[rows, :]
            gate[rows, :] += mm(x, wg_ref[...])
            up[rows, :] += mm(x, wu_ref[...])
            hid[rows, :] += mm(g_ref[rows, :], wd_ref[...], NT)

    @pl.when(i == steps - 1)
    def _():
        @pl.loop(0, count * 2)
        def _(c):
            rows = pl.ds(pl.multiple_of(c * (chunk // 2), chunk // 2), chunk // 2)
            g, u, d = gate[rows, :], up[rows, :], hid[rows, :]
            sig = jax.nn.sigmoid(g)
            silu = g * sig
            h_ref[rows, :] = (silu * u).astype(BF16)
            gg_ref[rows, :] = (d * u * (sig * (1.0 + g * (1.0 - sig)))).astype(BF16)
            ug_ref[rows, :] = (d * silu).astype(BF16)

    @pl.when(i >= steps)
    def _():
        @pl.loop(0, count)
        def _(c):
            rows = pl.ds(pl.multiple_of(c * chunk, chunk), chunk)
            ret_ref[rows, :] = (
                mm(gg_ref[rows, :], wg_ref[...], NT) + mm(ug_ref[rows, :], wu_ref[...], NT)
            ).astype(BF16)


def weights_body(r_ref, g_ref, h_ref, gg_ref, ug_ref, dg_ref, du_ref, dd_ref):
    width = r_ref.shape[1]
    chunk = 256

    @pl.loop(0, width // chunk)
    def _(c):
        cols = pl.ds(pl.multiple_of(c * chunk, chunk), chunk)
        x = r_ref[:, cols]
        dg_ref[cols, :] = mm(x, gg_ref[...], TN).astype(BF16)
        du_ref[cols, :] = mm(x, ug_ref[...], TN).astype(BF16)
        dd_ref[:, cols] = mm(h_ref[...], g_ref[:, cols], TN).astype(BF16)


def combine_body(head, scaling, mt_ref, ret_ref, og_ref, q_ref, ag_ref, lg_ref):
    width = og_ref.shape[1]
    rows = ret_ref.shape[1]
    total = og_ref[...].astype(F32)
    for p in range(2):
        both = (ret_ref[2 * p].astype(F32) + ret_ref[2 * p + 1].astype(F32)).astype(BF16)
        total = total + mm(mt_ref[:, p * rows : (p + 1) * rows], both)
    grad = total.astype(BF16)
    ag_ref[...] = grad
    for h in range(width // head):
        cols = slice(h * head, (h + 1) * head)
        lg_ref[cols, :] = (scaling * mm(q_ref[:, cols], grad[:, cols], TN)).astype(BF16)


def back_body(head, scaling, q_ref, mk_ref, v_ref, ag_ref, s_ref, gq_ref, gk_ref, gv_ref):
    length, width = q_ref.shape
    t = lax.broadcasted_iota(jnp.int32, (length, length), 0)
    s = lax.broadcasted_iota(jnp.int32, (length, length), 1)
    for h in range(width // head):
        cols = slice(h * head, (h + 1) * head)
        q, mk, v, ag = q_ref[:, cols], mk_ref[:, cols], v_ref[:, cols], ag_ref[:, cols]
        back = jnp.where(t >= s, mm(ag, v, NT), 0.0).astype(BF16)
        gq_ref[:, cols] = (scaling * (mm(back, mk) + mm(ag, s_ref[cols, :], NT))).astype(BF16)
        back = jnp.where(s >= t, mm(v, ag, NT), 0.0).astype(BF16)
        gk_ref[:, cols] = scaling * mm(back, q)
        scores = jnp.where(s >= t, mm(mk, q, NT), 0.0).astype(BF16)
        gv_ref[:, cols] = scaling * mm(scores, ag)


def final_body(head, mk_ref, v_ref, s_ref, g_ref, gki_ref, gvi_ref, gk_ref, gv_ref):
    width = mk_ref.shape[1]
    gate = spike_columns(s_ref[...], pl.program_id(0), width, head)
    for h in range(width // head):
        cols = slice(h * head, (h + 1) * head)
        state = g_ref[cols, :]
        gk = gki_ref[:, cols] + mm(v_ref[:, cols], state, NT)
        gk_ref[:, cols] = (gate[:, cols] * gk).astype(BF16)
        gv_ref[:, cols] = (gvi_ref[:, cols] + mm(mk_ref[:, cols], state)).astype(BF16)


def shape(*dims, dtype=BF16):
    return jax.ShapeDtypeStruct(dims, dtype)


def on_device(
    queries,
    key_vectors,
    value_vectors,
    spikes,
    routes,
    route_probs,
    gate_weight,
    up_weight,
    down_weight,
    out_grad,
):
    length, width = queries.shape
    heads = spikes.shape[1]
    head = width // heads
    tokens, model = out_grad.shape
    top = routes.shape[1]
    ctx = lax.axis_size("ctx")
    exp = lax.axis_size("exp")
    devices = ctx * exp
    experts = devices // 2
    capacity = 2 * max(1, 3 * tokens * top // (4 * experts))
    scaling = 1.0 / math.sqrt(head * length * ctx)
    hidden = gate_weight.shape[2]
    slots = exp * capacity
    half_rows = ctx * slots
    rows = 2 * half_rows
    pair = 2 * head
    pairs = width // pair
    everywhere = ("exp", "ctx")

    def cols(n=1, m=1):
        return pl.BlockSpec((n, m), lambda i: (0, i))

    def whole(*dims):
        return pl.BlockSpec(dims, lambda i: (0,) * len(dims))

    tall = pl.BlockSpec((pair, head), lambda i: (i, 0))
    wide = cols(length, pair)
    seq = shape(length, width)
    seq32 = shape(length, width, dtype=F32)
    unit = length * width * 2

    def exchange(part, reverse):
        pieces = part.reshape(ctx, heads * head // ctx, head)
        pieces = lax.all_to_all(pieces, "ctx", 0, 0, tiled=True)
        pieces = call(
            functools.partial(sum_body, reverse), (1,),
            [whole(*pieces.shape)], whole(*pieces.shape), shape(*pieces.shape), 1e6, 1 << 19,
        )(pieces)
        return lax.all_to_all(pieces, "ctx", 0, 0, tiled=True).reshape(heads * head, head)

    block_state, masked = call(
        functools.partial(state_body, head), (pairs,),
        [wide, wide, whole(length, heads)], [tall, wide],
        [shape(heads * head, head), seq], 2 * length * width * head, 3 * unit,
    )(key_vectors, value_vectors, spikes)
    states_in = exchange(block_state, False)
    intra = call(
        functools.partial(intra_body, head), (pairs,), [wide] * 3, wide, seq32,
        4 * length * length * width, 5 * unit,
    )(queries, masked, value_vectors)

    place = lax.broadcasted_iota(jnp.int32, (tokens, tokens), 0)
    later = place < lax.broadcasted_iota(jnp.int32, (tokens, tokens), 1)
    r0, r1 = routes[:, 0], routes[:, 1]

    def target(own):
        same = (r0[:, None] == own[None, :]).astype(jnp.int32)
        same = same + (r1[:, None] == own[None, :]).astype(jnp.int32)
        slot = jnp.sum(jnp.where(later, same, 0), axis=0)
        row = (own % 2) * half_rows + (own // 2) * slots + lax.axis_index("exp") * capacity
        return (row + slot).astype(F32)

    pack = jnp.stack(
        [target(r0), target(r1), route_probs[:, 0].astype(F32), route_probs[:, 1].astype(F32)]
    )
    pack = lax.all_gather(pack, "exp")
    select, weigh, select_t = call(
        select_body, (exp,), [pl.BlockSpec((1, 4, tokens), lambda i: (i, 0, 0))],
        [cols(rows, tokens), cols(rows, tokens), pl.BlockSpec((tokens, rows), lambda i: (i, 0))],
        [shape(rows, length), shape(rows, length), shape(length, rows)],
        1e6, 6 * rows * length,
    )(pack)

    grad_cols = lax.all_to_all(
        out_grad.reshape(tokens, exp, width).transpose(1, 0, 2), "exp", 0, 0, tiled=True
    ).reshape(length, width)
    send_shape = shape(2, 2, half_rows, 2 * width)
    send_flops = 2 * rows * length * width
    send_bytes = 4 * rows * width + 2 * rows * length + 2 * unit
    buffer = call(
        grads_body, (pairs,), [whole(rows, length), wide],
        pl.BlockSpec((2, 2, half_rows, pair), lambda i: (0, 0, 0, i + pairs)),
        send_shape, send_flops, send_bytes,
    )(weigh, grad_cols)
    buffer = call(
        functools.partial(rows_body, head, scaling), (pairs,),
        [whole(rows, length), wide, wide, tall, pl.BlockSpec(memory_space=pl.ANY)],
        pl.BlockSpec((2, 2, half_rows, pair), lambda i: (0, 0, 0, i)),
        send_shape, send_flops, send_bytes, input_output_aliases={4: 0},
    )(select, queries, intra, states_in, buffer)
    got = lax.all_to_all(
        buffer.reshape(devices, slots, 2 * width), everywhere, 0, 0, tiled=True
    ).reshape(exp * half_rows, 2 * width)

    gate_local, up_local, down_local = gate_weight[0], up_weight[0], down_weight[0]
    act = shape(half_rows, hidden)
    last = exp - 1
    block = half_rows * width * 2
    back_rows, hid, gate_grad, up_grad = call(
        functools.partial(expert_body, exp, 256), (2 * exp,),
        [
            pl.BlockSpec((half_rows, width), lambda i: (jnp.minimum(i, last), 0)),
            pl.BlockSpec((half_rows, width), lambda i: (jnp.minimum(i, last), 1)),
            pl.BlockSpec((width, hidden), lambda i: (i % exp, 0)),
            pl.BlockSpec((width, hidden), lambda i: (i % exp, 0)),
            pl.BlockSpec((hidden, width), lambda i: (0, jnp.minimum(i, last))),
        ],
        [
            pl.BlockSpec((half_rows, width), lambda i: (jnp.maximum(i - exp, 0), 0)),
            *[whole(half_rows, hidden)] * 3,
        ],
        [shape(exp * half_rows, width), act, act, act],
        10 * half_rows * model * hidden, 12 * block + 10 * model * hidden, 52,
        scratch_shapes=[pltpu.VMEM((half_rows, hidden), F32)] * 3,
    )(got, got, gate_local, up_local, down_local)
    returned = lax.all_to_all(
        back_rows.reshape(devices, slots, width), everywhere, 0, 0, tiled=True
    ).reshape(exp, half_rows, width)
    grad_gate, grad_up, grad_down = call(
        weights_body, (exp,),
        [
            pl.BlockSpec((half_rows, width), lambda i: (i, 0)),
            pl.BlockSpec((half_rows, width), lambda i: (i, 1)),
            *[whole(half_rows, hidden)] * 3,
        ],
        [
            pl.BlockSpec((width, hidden), lambda i: (i, 0)),
            pl.BlockSpec((width, hidden), lambda i: (i, 0)),
            pl.BlockSpec((hidden, width), lambda i: (0, i)),
        ],
        [shape(model, hidden), shape(model, hidden), shape(hidden, model)],
        6 * half_rows * model * hidden, 8 * block + 6 * model * hidden, 40,
    )(got, got, hid, gate_grad, up_grad)

    att_grad, local_grad = call(
        functools.partial(combine_body, head, scaling), (pairs,),
        [whole(length, rows), pl.BlockSpec((exp, half_rows, pair), lambda i: (0, 0, i)), wide, wide],
        [wide, tall], [seq, shape(heads * head, head)],
        2 * rows * length * width, 2 * rows * length + 4 * block + 3 * unit,
    )(select_t, returned, grad_cols, queries)
    grad_states = exchange(local_grad, True)
    grad_queries, keys_part, values_part = call(
        functools.partial(back_body, head, scaling), (pairs,), [wide] * 4 + [tall], [wide] * 3,
        [seq, seq32, seq32], 12 * length * length * width, 9 * unit,
    )(queries, masked, value_vectors, att_grad, states_in)
    grad_keys, grad_values = call(
        functools.partial(final_body, head), (pairs,),
        [wide, wide, whole(length, heads), tall, wide, wide], [wide] * 2, [seq, seq],
        4 * length * width * head, 8 * unit,
    )(masked, value_vectors, spikes, grad_states, keys_part, values_part)
    return grad_queries, grad_keys, grad_values, grad_gate[None], grad_up[None], grad_down[None]


def solution(mesh):
    by_head = P("ctx", "exp")
    by_device = P(("ctx", "exp"), None)
    by_half = P(("ctx", "exp"), None, None)
    return jax.shard_map(
        on_device,
        mesh=mesh,
        in_specs=(by_head,) * 4 + (by_device,) * 2 + (by_half,) * 3 + (by_device,),
        out_specs=(by_head,) * 3 + (by_half,) * 3,
        check_vma=False,
    )
```

```python
import functools
import math

import jax
import jax.numpy as jnp
from jax import lax
from jax.experimental import pallas as pl
from jax.experimental.pallas import tpu as pltpu
from jax.sharding import PartitionSpec as P

F32 = jnp.float32
BF16 = jnp.bfloat16
NN = (((1,), (0,)), ((), ()))
NT = (((1,), (1,)), ((), ()))
TN = (((0,), (0,)), ((), ()))


def mm(a, b, dims=NN):
    return lax.dot_general(a, b, dims, preferred_element_type=F32)


def call(body, grid, in_specs, out_specs, out_shape, flops, nbytes, vmem=60, **kw):
    return pl.pallas_call(
        body,
        grid=grid,
        in_specs=in_specs,
        out_specs=out_specs,
        out_shape=out_shape,
        compiler_params=pltpu.CompilerParams(
            dimension_semantics=("arbitrary",) * len(grid), vmem_limit_bytes=vmem << 20
        ),
        cost_estimate=pl.CostEstimate(
            flops=int(flops), bytes_accessed=int(nbytes), transcendentals=0
        ),
        **kw,
    )


def spike_columns(spikes, pair, width, head):
    heads = spikes.shape[1]
    col = lax.broadcasted_iota(jnp.int32, (heads, width), 1) // head + pair * (width // head)
    row = lax.broadcasted_iota(jnp.int32, (heads, width), 0)
    spread = jnp.where(col == row, 1.0, 0.0).astype(BF16)
    return mm(spikes.astype(F32).astype(BF16), spread)


def cut_body(capacity, slots, half_rows, mine_ref, x_ref, r_ref, p_ref, *o_refs):
    width = o_refs[0].shape[1]
    tokens = x_ref.shape[0]
    extra = o_refs[0].shape[0] - tokens
    row = lax.broadcasted_iota(jnp.int32, (tokens, tokens), 0)
    col = lax.broadcasted_iota(jnp.int32, (tokens, tokens), 1)

    def lanes(column):
        return jnp.sum(jnp.where(row == col, column, 0.0), axis=0, keepdims=True)

    named = r_ref[...].astype(F32)
    probs = p_ref[...].astype(F32)
    line = lax.broadcasted_iota(jnp.int32, (extra, tokens), 0)
    pack = jnp.zeros((extra, tokens), F32)
    for k in range(2):
        expert = lanes(named[:, k : k + 1])
        same = jnp.where(named[:, 0:1] == expert, 1.0, 0.0)
        same = same + jnp.where(named[:, 1:2] == expert, 1.0, 0.0)
        slot = jnp.sum(jnp.where(row < col, same, 0.0), axis=0, keepdims=True)
        half = jnp.floor(expert * 0.5)
        place = (expert - 2.0 * half) * half_rows + half * slots + slot
        place = place + (mine_ref[0] * capacity).astype(F32)
        high = jnp.floor(place * 0.125)
        for at, value in (
            (3 * k, high), (3 * k + 1, place - 8.0 * high), (3 * k + 2, lanes(probs[:, k : k + 1]))
        ):
            pack = jnp.where(line == at, value, pack)
    for i, o_ref in enumerate(o_refs):
        at = lax.rem(mine_ref[0] + i, len(o_refs)) * width
        o_ref[:tokens, :] = x_ref[:, pl.ds(pl.multiple_of(at, width), width)]
        o_ref[tokens:, :] = jnp.zeros((extra, width), BF16)
        o_ref[tokens:, :tokens] = pack.astype(BF16)


def prepare_body(count, mine_ref, *refs):
    x_refs, (g_ref, m_ref, mt_ref, o_ref, w_ref) = refs[:count], refs[count:]
    rows = m_ref.shape[0]
    tokens = g_ref.shape[0] // count
    pair = o_ref.shape[3]
    step = pl.program_id(0)

    @pl.when(step == 0)
    def _():
        down = lax.broadcasted_iota(jnp.int32, (rows, tokens), 0).astype(F32)
        across = lax.broadcasted_iota(jnp.int32, (tokens, rows), 1).astype(F32)
        eye = lax.broadcasted_iota(jnp.int32, (tokens, tokens), 0) == lax.broadcasted_iota(
            jnp.int32, (tokens, tokens), 1
        )
        for i, x_ref in enumerate(x_refs):
            at = pl.multiple_of(lax.rem(mine_ref[0] + count - i, count) * tokens, tokens)
            g_ref[pl.ds(at, tokens), :] = x_ref[:tokens, :]
            pack = x_ref[tokens:, :tokens].astype(F32)
            first = 8.0 * pack[0:1] + pack[1:2]
            second = 8.0 * pack[3:4] + pack[4:5]
            hit0, hit1 = down == first, down == second
            m_ref[:, pl.ds(at, tokens)] = jnp.where(hit0 | hit1, 1.0, 0.0).astype(BF16)
            w_ref[:, pl.ds(at, tokens)] = jnp.where(
                hit0, pack[2:3], jnp.where(hit1, pack[5:6], 0.0)
            ).astype(BF16)
            first = jnp.sum(jnp.where(eye, first, 0.0), axis=1, keepdims=True)
            second = jnp.sum(jnp.where(eye, second, 0.0), axis=1, keepdims=True)
            mt_ref[pl.ds(at, tokens), :] = jnp.where(
                (across == first) | (across == second), 1.0, 0.0
            ).astype(BF16)

    @pl.when(step > 0)
    def _():
        cols = pl.ds(pl.multiple_of((step - 1) * pair, pair), pair)
        put_rows(w_ref, g_ref[:, cols], o_ref)


def state_body(head, k_ref, v_ref, s_ref, bs_ref, mk_ref):
    width = k_ref.shape[1]
    gate = spike_columns(s_ref[...], pl.program_id(0), width, head)
    masked = (k_ref[...].astype(F32) * gate).astype(BF16)
    mk_ref[...] = masked
    value = v_ref[...]
    for h in range(width // head):
        cols = slice(h * head, (h + 1) * head)
        bs_ref[cols, :] = mm(masked[:, cols], value[:, cols], TN).astype(BF16)


def intra_body(head, q_ref, mk_ref, v_ref, o_ref):
    length, width = q_ref.shape
    t = lax.broadcasted_iota(jnp.int32, (length, length), 0)
    s = lax.broadcasted_iota(jnp.int32, (length, length), 1)
    for h in range(width // head):
        cols = slice(h * head, (h + 1) * head)
        scores = mm(q_ref[:, cols], mk_ref[:, cols], NT)
        scores = jnp.where(t >= s, scores, 0.0).astype(BF16)
        o_ref[:, cols] = mm(scores, v_ref[:, cols])


def sum_body(reverse, x_ref, o_ref):
    count = x_ref.shape[0]

    def step(i, total):
        at = count - 1 - i if reverse else i
        o_ref[at] = total.astype(BF16)
        return total + x_ref[at].astype(F32)

    lax.fori_loop(0, count, step, jnp.zeros(x_ref.shape[1:], F32))


def put_rows(m_ref, columns, o_ref):
    rows = o_ref.shape[2]
    for p in range(2):
        picked = mm(m_ref[p * rows : (p + 1) * rows, :], columns).astype(BF16)
        o_ref[p, 0] = picked
        o_ref[p, 1] = picked


def rows_body(head, scaling, m_ref, q_ref, intra_ref, s_ref, buf_ref, o_ref):
    del buf_ref
    width = q_ref.shape[1]
    parts = []
    for h in range(width // head):
        cols = slice(h * head, (h + 1) * head)
        inter = mm(q_ref[:, cols], s_ref[cols, :])
        parts.append((scaling * (intra_ref[:, cols] + inter)).astype(BF16))
    put_rows(m_ref, jnp.concatenate(parts, axis=1), o_ref)


def expert_body(
    steps, r_ref, g_ref, wg_ref, wu_ref, wd_ref, ret_ref, h_ref, a_ref, gate, up, hid
):
    i = pl.program_id(0)
    rows, width = hid.shape
    chunk = rows // 6

    @pl.when(i == 0)
    def _():
        gate[...] = mm(r_ref[...], wg_ref[...])
        up[...] = mm(r_ref[...], wu_ref[...])
        hid[...] = mm(g_ref[...], wd_ref[...], NT)

    @pl.when((i > 0) & (i < steps))
    def _():
        gate[...] += mm(r_ref[...], wg_ref[...])
        up[...] += mm(r_ref[...], wu_ref[...])
        hid[...] += mm(g_ref[...], wd_ref[...], NT)

    @pl.when(i == steps - 1)
    def _():
        @pl.loop(0, rows // chunk)
        def _(c):
            part = pl.ds(pl.multiple_of(c * chunk, chunk), chunk)
            g, u, d = gate[part, :], up[part, :], hid[part, :]
            sig = jax.nn.sigmoid(g)
            silu = g * sig
            h_ref[part, :] = (silu * u).astype(BF16)
            a_ref[part, :width] = (d * u * (sig * (1.0 + g * (1.0 - sig)))).astype(BF16)
            a_ref[part, width:] = (d * silu).astype(BF16)

    @pl.when(i >= steps)
    def _():
        ret_ref[...] = (
            mm(a_ref[:, :width], wg_ref[...], NT) + mm(a_ref[:, width:], wu_ref[...], NT)
        ).astype(BF16)


def weights_body(r_ref, g_ref, h_ref, a_ref, dg_ref, du_ref, dd_ref):
    width = r_ref.shape[1]
    hidden = h_ref.shape[1]
    chunk = 256

    @pl.loop(0, width // chunk)
    def _(c):
        cols = pl.ds(pl.multiple_of(c * chunk, chunk), chunk)
        both = mm(r_ref[:, cols], a_ref[...], TN)
        dg_ref[cols, :] = both[:, :hidden].astype(BF16)
        du_ref[cols, :] = both[:, hidden:].astype(BF16)
        dd_ref[:, cols] = mm(h_ref[...], g_ref[:, cols], TN).astype(BF16)


def combine_body(head, scaling, mt_ref, ret_ref, og_ref, q_ref, ag_ref, lg_ref):
    width = og_ref.shape[1]
    rows = ret_ref.shape[1]
    total = og_ref[...].astype(F32)
    for p in range(2):
        both = (ret_ref[2 * p].astype(F32) + ret_ref[2 * p + 1].astype(F32)).astype(BF16)
        total = total + mm(mt_ref[:, p * rows : (p + 1) * rows], both)
    grad = total.astype(BF16)
    ag_ref[...] = grad
    for h in range(width // head):
        cols = slice(h * head, (h + 1) * head)
        lg_ref[cols, :] = (scaling * mm(q_ref[:, cols], grad[:, cols], TN)).astype(BF16)


def back_query_body(head, scaling, mk_ref, v_ref, ag_ref, s_ref, gq_ref):
    length, width = mk_ref.shape
    t = lax.broadcasted_iota(jnp.int32, (length, length), 0)
    s = lax.broadcasted_iota(jnp.int32, (length, length), 1)
    for h in range(width // head):
        cols = slice(h * head, (h + 1) * head)
        ag = ag_ref[:, cols]
        back = jnp.where(t >= s, mm(ag, v_ref[:, cols], NT), 0.0).astype(BF16)
        total = mm(back, mk_ref[:, cols]) + mm(ag, s_ref[cols, :], NT)
        gq_ref[:, cols] = (scaling * total).astype(BF16)


def back_body(head, scaling, q_ref, mk_ref, v_ref, ag_ref, gk_ref, gv_ref):
    length, width = q_ref.shape
    s = lax.broadcasted_iota(jnp.int32, (length, length), 0)
    t = lax.broadcasted_iota(jnp.int32, (length, length), 1)
    for h in range(width // head):
        cols = slice(h * head, (h + 1) * head)
        q, ag = q_ref[:, cols], ag_ref[:, cols]
        back = jnp.where(t >= s, mm(v_ref[:, cols], ag, NT), 0.0).astype(BF16)
        gk_ref[:, cols] = scaling * mm(back, q)
        scores = jnp.where(t >= s, mm(mk_ref[:, cols], q, NT), 0.0).astype(BF16)
        gv_ref[:, cols] = scaling * mm(scores, ag)


def final_body(head, mk_ref, v_ref, s_ref, g_ref, gki_ref, gvi_ref, gk_ref, gv_ref):
    width = mk_ref.shape[1]
    gate = spike_columns(s_ref[...], pl.program_id(0), width, head)
    for h in range(width // head):
        cols = slice(h * head, (h + 1) * head)
        state = g_ref[cols, :]
        gk = gki_ref[:, cols] + mm(v_ref[:, cols], state, NT)
        gk_ref[:, cols] = (gate[:, cols] * gk).astype(BF16)
        gv_ref[:, cols] = (gvi_ref[:, cols] + mm(mk_ref[:, cols], state)).astype(BF16)


def shape(*dims, dtype=BF16):
    return jax.ShapeDtypeStruct(dims, dtype)


def on_device(
    queries,
    key_vectors,
    value_vectors,
    spikes,
    routes,
    route_probs,
    gate_weight,
    up_weight,
    down_weight,
    out_grad,
):
    length, width = queries.shape
    heads = spikes.shape[1]
    head = width // heads
    tokens, model = out_grad.shape
    top = routes.shape[1]
    ctx = lax.axis_size("ctx")
    exp = lax.axis_size("exp")
    devices = ctx * exp
    experts = devices // 2
    capacity = 2 * max(1, 3 * tokens * top // (4 * experts))
    scaling = 1.0 / math.sqrt(head * length * ctx)
    hidden = gate_weight.shape[2]
    slots = exp * capacity
    half_rows = ctx * slots
    rows = 2 * half_rows
    pair = 2 * head
    pairs = width // pair
    everywhere = ("exp", "ctx")

    def cols(n=1, m=1):
        return pl.BlockSpec((n, m), lambda i: (0, i))

    def whole(*dims):
        return pl.BlockSpec(dims, lambda i: (0,) * len(dims))

    tall = pl.BlockSpec((pair, head), lambda i: (i, 0))
    wide = cols(length, pair)
    seq = shape(length, width)
    seq32 = shape(length, width, dtype=F32)
    unit = length * width * 2

    def exchange(part, reverse, cover):
        pieces = part.reshape(ctx, heads * head // ctx, head)
        pieces = lax.all_to_all(pieces, "ctx", 0, 0, tiled=True)
        pieces, cover = lax.optimization_barrier((pieces, cover))
        pieces = call(
            functools.partial(sum_body, reverse), (1,),
            [whole(*pieces.shape)], whole(*pieces.shape), shape(*pieces.shape), 1e6, 1 << 19, 4,
        )(pieces)
        pieces = lax.all_to_all(pieces, "ctx", 0, 0, tiled=True)
        return pieces.reshape(heads * head, head), cover

    block_state, masked = call(
        functools.partial(state_body, head), (pairs,),
        [wide, wide, whole(length, heads)], [tall, wide],
        [shape(heads * head, head), seq], 2 * length * width * head, 3 * unit,
    )(key_vectors, value_vectors, spikes)
    mine = lax.axis_index("exp").reshape(1)
    smem = pl.BlockSpec(memory_space=pltpu.SMEM)
    piece = (tokens + 16, width)
    pieces = call(
        functools.partial(cut_body, capacity, slots, half_rows), (1,),
        [smem, whole(tokens, model), whole(tokens, top), whole(tokens, top)],
        [whole(*piece)] * exp, [shape(*piece)] * exp, 1e6, 2 * unit,
    )(mine, out_grad, routes, route_probs)
    pieces, block_state = lax.optimization_barrier((tuple(pieces), block_state))
    pieces = [pieces[0]] + [
        lax.ppermute(pieces[i], "exp", [(j, (j + i) % exp) for j in range(exp)])
        for i in range(1, exp)
    ]
    states_in, _ = exchange(block_state, False, ())
    intra = call(
        functools.partial(intra_body, head), (pairs,), [wide] * 3, wide, seq32,
        4 * length * length * width, 5 * unit,
    )(queries, masked, value_vectors)

    send_shape = shape(2, 2, half_rows, 2 * width)
    send_flops = 2 * rows * length * width
    send_bytes = 4 * rows * width + 2 * rows * length + 2 * unit
    grad_cols, select, select_t, buffer = call(
        functools.partial(prepare_body, exp), (1 + pairs,), [smem] + [whole(*piece)] * exp,
        [
            whole(length, width), whole(rows, length), whole(length, rows),
            pl.BlockSpec(
                (2, 2, half_rows, pair), lambda i: (0, 0, 0, jnp.maximum(i - 1, 0) + pairs)
            ),
        ],
        [seq, shape(rows, length), shape(length, rows), send_shape], send_flops, send_bytes,
        scratch_shapes=[pltpu.VMEM((rows, length), BF16)],
    )(mine, *pieces)
    buffer = call(
        functools.partial(rows_body, head, scaling), (pairs,),
        [whole(rows, length), wide, wide, tall, pl.BlockSpec(memory_space=pl.ANY)],
        pl.BlockSpec((2, 2, half_rows, pair), lambda i: (0, 0, 0, i)),
        send_shape, send_flops, send_bytes, input_output_aliases={4: 0},
    )(select, queries, intra, states_in, buffer)
    got = lax.all_to_all(
        buffer.reshape(devices, slots, 2 * width), everywhere, 0, 0, tiled=True
    ).reshape(exp * half_rows, 2 * width)

    act = shape(half_rows, hidden)
    last = exp - 1
    block = half_rows * width * 2
    back_rows, hid, acts = call(
        functools.partial(expert_body, exp), (2 * exp,),
        [
            pl.BlockSpec((half_rows, width), lambda i: (jnp.minimum(i, last), 0)),
            pl.BlockSpec((half_rows, width), lambda i: (jnp.minimum(i, last), 1)),
            pl.BlockSpec((width, hidden), lambda i: (i % exp, 0)),
            pl.BlockSpec((width, hidden), lambda i: (i % exp, 0)),
            pl.BlockSpec((hidden, width), lambda i: (0, jnp.minimum(i, last))),
        ],
        [
            pl.BlockSpec((half_rows, width), lambda i: (jnp.maximum(i - exp, 0), 0)),
            whole(half_rows, hidden),
            whole(half_rows, 2 * hidden),
        ],
        [shape(exp * half_rows, width), act, shape(half_rows, 2 * hidden)],
        10 * half_rows * model * hidden, 12 * block + 10 * model * hidden,
        scratch_shapes=[pltpu.VMEM((half_rows, hidden), F32)] * 3,
    )(got, got, gate_weight[0], up_weight[0], down_weight[0])
    returned = lax.all_to_all(
        back_rows.reshape(devices, slots, width), everywhere, 0, 0, tiled=True
    ).reshape(exp, half_rows, width)
    grad_gate, grad_up, grad_down = call(
        weights_body, (exp,),
        [
            pl.BlockSpec((half_rows, width), lambda i: (i, 0)),
            pl.BlockSpec((half_rows, width), lambda i: (i, 1)),
            whole(half_rows, hidden),
            whole(half_rows, 2 * hidden),
        ],
        [
            pl.BlockSpec((width, hidden), lambda i: (i, 0)),
            pl.BlockSpec((width, hidden), lambda i: (i, 0)),
            pl.BlockSpec((hidden, width), lambda i: (0, i)),
        ],
        [shape(model, hidden), shape(model, hidden), shape(hidden, model)],
        6 * half_rows * model * hidden, 8 * block + 6 * model * hidden,
    )(got, got, hid, acts)

    returned, grad_gate, grad_up, grad_down = lax.optimization_barrier(
        (returned, grad_gate, grad_up, grad_down)
    )

    att_grad, local_grad = call(
        functools.partial(combine_body, head, scaling), (pairs,),
        [whole(length, rows), pl.BlockSpec((exp, half_rows, pair), lambda i: (0, 0, i)), wide, wide],
        [wide, tall], [seq, shape(heads * head, head)],
        2 * rows * length * width, 2 * rows * length + 4 * block + 3 * unit,
    )(select_t, returned, grad_cols, queries)
    parts = call(
        functools.partial(back_body, head, scaling), (pairs,), [wide] * 4, [wide] * 2,
        [seq32, seq32], 8 * length * length * width, 8 * unit,
    )(queries, masked, value_vectors, att_grad)
    grad_states, (keys_part, values_part) = exchange(local_grad, True, tuple(parts))
    grad_queries = call(
        functools.partial(back_query_body, head, scaling), (pairs,), [wide] * 3 + [tall], wide, seq,
        4 * length * length * width, 4 * unit,
    )(masked, value_vectors, att_grad, states_in)
    grad_keys, grad_values = call(
        functools.partial(final_body, head), (pairs,),
        [wide, wide, whole(length, heads), tall, wide, wide], [wide] * 2, [seq, seq],
        4 * length * width * head, 8 * unit,
    )(masked, value_vectors, spikes, grad_states, keys_part, values_part)
    return grad_queries, grad_keys, grad_values, grad_gate[None], grad_up[None], grad_down[None]


def solution(mesh):
    by_head = P("ctx", "exp")
    by_device = P(("ctx", "exp"), None)
    by_half = P(("ctx", "exp"), None, None)
    return jax.shard_map(
        on_device,
        mesh=mesh,
        in_specs=(by_head,) * 4 + (by_device,) * 2 + (by_half,) * 3 + (by_device,),
        out_specs=(by_head,) * 3 + (by_half,) * 3,
        check_vma=False,
    )
```

```python
import functools
import math

import jax
import jax.numpy as jnp
from jax import lax
from jax.experimental import pallas as pl
from jax.experimental.pallas import tpu as pltpu
from jax.sharding import PartitionSpec as P

F32 = jnp.float32
BF16 = jnp.bfloat16
NN = (((1,), (0,)), ((), ()))
NT = (((1,), (1,)), ((), ()))
TN = (((0,), (0,)), ((), ()))


def mm(a, b, dims=NN):
    return lax.dot_general(a, b, dims, preferred_element_type=F32)


def call(body, grid, in_specs, out_specs, out_shape, flops, nbytes, vmem=60, **kw):
    return pl.pallas_call(
        body,
        grid=grid,
        in_specs=in_specs,
        out_specs=out_specs,
        out_shape=out_shape,
        compiler_params=pltpu.CompilerParams(
            dimension_semantics=("arbitrary",) * len(grid), vmem_limit_bytes=vmem << 20
        ),
        cost_estimate=pl.CostEstimate(
            flops=int(flops), bytes_accessed=int(nbytes), transcendentals=0
        ),
        **kw,
    )


def spike_columns(spikes, pair, width, head):
    heads = spikes.shape[0]
    col = lax.broadcasted_iota(jnp.int32, (heads, width), 1) // head + pair * (width // head)
    row = lax.broadcasted_iota(jnp.int32, (heads, width), 0)
    spread = jnp.where(col == row, 1.0, 0.0).astype(BF16)
    return mm(spikes.astype(F32).astype(BF16), spread, TN)


def cut_body(capacity, slots, half_rows, mine_ref, x_ref, r_ref, p_ref, *o_refs):
    width = o_refs[0].shape[1]
    tokens = x_ref.shape[0]
    extra = o_refs[0].shape[0] - tokens
    row = lax.broadcasted_iota(jnp.int32, (tokens, tokens), 0)
    col = lax.broadcasted_iota(jnp.int32, (tokens, tokens), 1)

    def column(lanes):
        return jnp.sum(jnp.where(row == col, lanes, 0.0), axis=1, keepdims=True)

    named = r_ref[...].astype(F32)
    probs = p_ref[...].astype(F32)
    line = lax.broadcasted_iota(jnp.int32, (extra, tokens), 0)
    pack = jnp.zeros((extra, tokens), F32)
    first, second = column(named[0:1, :]), column(named[1:2, :])
    for k in range(2):
        expert = named[k : k + 1, :]
        same = jnp.where(first == expert, 1.0, 0.0) + jnp.where(second == expert, 1.0, 0.0)
        slot = jnp.sum(jnp.where(row < col, same, 0.0), axis=0, keepdims=True)
        half = jnp.floor(expert * 0.5)
        place = (expert - 2.0 * half) * half_rows + half * slots + slot
        place = place + (mine_ref[0] * capacity).astype(F32)
        high = jnp.floor(place * 0.125)
        for at, value in (
            (3 * k, high), (3 * k + 1, place - 8.0 * high), (3 * k + 2, probs[k : k + 1, :])
        ):
            pack = jnp.where(line == at, value, pack)
    for i, o_ref in enumerate(o_refs):
        at = lax.rem(mine_ref[0] + i, len(o_refs)) * width
        o_ref[:tokens, :] = x_ref[:, pl.ds(pl.multiple_of(at, width), width)]
        o_ref[tokens:, :] = jnp.zeros((extra, width), BF16)
        o_ref[tokens:, :tokens] = pack.astype(BF16)


def prepare_body(count, mine_ref, *refs):
    x_refs, (g_ref, m_ref, o_ref, w_ref) = refs[:count], refs[count:]
    rows = m_ref.shape[0]
    tokens = g_ref.shape[0] // count
    pair = o_ref.shape[3]
    step = pl.program_id(0)

    @pl.when(step == 0)
    def _():
        down = lax.broadcasted_iota(jnp.int32, (rows, tokens), 0).astype(F32)
        for i, x_ref in enumerate(x_refs):
            at = pl.multiple_of(lax.rem(mine_ref[0] + count - i, count) * tokens, tokens)
            g_ref[pl.ds(at, tokens), :] = x_ref[:tokens, :]
            pack = x_ref[tokens:, :tokens].astype(F32)
            first = 8.0 * pack[0:1] + pack[1:2]
            second = 8.0 * pack[3:4] + pack[4:5]
            hit0, hit1 = down == first, down == second
            m_ref[:, pl.ds(at, tokens)] = jnp.where(hit0 | hit1, 1.0, 0.0).astype(BF16)
            w_ref[:, pl.ds(at, tokens)] = jnp.where(
                hit0, pack[2:3], jnp.where(hit1, pack[5:6], 0.0)
            ).astype(BF16)

    @pl.when(step > 0)
    def _():
        cols = pl.ds(pl.multiple_of((step - 1) * pair, pair), pair)
        put_rows(w_ref, g_ref[:, cols], o_ref)


def state_body(head, k_ref, v_ref, s_ref, bs_ref, mk_ref):
    width = k_ref.shape[1]
    gate = spike_columns(s_ref[...], pl.program_id(0), width, head)
    masked = (k_ref[...].astype(F32) * gate).astype(BF16)
    mk_ref[...] = masked
    value = v_ref[...]
    for h in range(width // head):
        cols = slice(h * head, (h + 1) * head)
        bs_ref[cols, :] = mm(masked[:, cols], value[:, cols], TN).astype(BF16)


def sum_body(reverse, x_ref, o_ref):
    count = x_ref.shape[0]

    def step(i, total):
        at = count - 1 - i if reverse else i
        o_ref[at] = total.astype(BF16)
        return total + x_ref[at].astype(F32)

    lax.fori_loop(0, count, step, jnp.zeros(x_ref.shape[1:], F32))


def select_t_body(count, mine_ref, *refs):
    x_refs, mt_ref = refs[:count], refs[count]
    rows = mt_ref.shape[1]
    tokens = mt_ref.shape[0] // count
    across = lax.broadcasted_iota(jnp.int32, (tokens, rows), 1).astype(F32)
    eye = lax.broadcasted_iota(jnp.int32, (tokens, tokens), 0) == lax.broadcasted_iota(
        jnp.int32, (tokens, tokens), 1
    )
    for i, x_ref in enumerate(x_refs):
        at = pl.multiple_of(lax.rem(mine_ref[0] + count - i, count) * tokens, tokens)
        pack = x_ref[tokens:, :tokens].astype(F32)
        first, second = 8.0 * pack[0:1] + pack[1:2], 8.0 * pack[3:4] + pack[4:5]
        first = jnp.sum(jnp.where(eye, first, 0.0), axis=1, keepdims=True)
        second = jnp.sum(jnp.where(eye, second, 0.0), axis=1, keepdims=True)
        mt_ref[pl.ds(at, tokens), :] = jnp.where(
            (across == first) | (across == second), 1.0, 0.0
        ).astype(BF16)


def put_rows(m_ref, columns, o_ref):
    rows = o_ref.shape[2]
    for p in range(2):
        picked = mm(m_ref[p * rows : (p + 1) * rows, :], columns).astype(BF16)
        o_ref[p, 0] = picked
        o_ref[p, 1] = picked


def rows_body(head, scaling, m_ref, q_ref, mk_ref, v_ref, s_ref, buf_ref, o_ref):
    del buf_ref
    length, width = q_ref.shape
    t = lax.broadcasted_iota(jnp.int32, (length, length), 0)
    s = lax.broadcasted_iota(jnp.int32, (length, length), 1)
    parts = []
    for h in range(width // head):
        cols = slice(h * head, (h + 1) * head)
        scores = mm(q_ref[:, cols], mk_ref[:, cols], NT)
        scores = jnp.where(t >= s, scores, 0.0).astype(BF16)
        total = mm(scores, v_ref[:, cols]) + mm(q_ref[:, cols], s_ref[cols, :])
        parts.append((scaling * total).astype(BF16))
    put_rows(m_ref, jnp.concatenate(parts, axis=1), o_ref)


def expert_body(
    steps, r_ref, g_ref, wg_ref, wu_ref, wd_ref, ret_ref, h_ref, a_ref, both, hid, cat
):
    i = pl.program_id(0)
    rows, hidden = hid.shape
    width = r_ref.shape[1]
    chunk = rows // 6
    part = pl.ds(pl.multiple_of(lax.rem(i, steps) * width, width), width)

    @pl.when(i < steps)
    def _():
        cat[part, :hidden] = wg_ref[...]
        cat[part, hidden:] = wu_ref[...]

    @pl.when(i == 0)
    def _():
        both[...] = mm(r_ref[...], cat[part, :])
        hid[...] = mm(g_ref[...], wd_ref[...], NT)

    @pl.when((i > 0) & (i < steps))
    def _():
        both[...] += mm(r_ref[...], cat[part, :])
        hid[...] += mm(g_ref[...], wd_ref[...], NT)

    @pl.when(i == steps - 1)
    def _():
        @pl.loop(0, rows // chunk)
        def _(c):
            at = pl.ds(pl.multiple_of(c * chunk, chunk), chunk)
            g, u, d = both[at, :hidden], both[at, hidden:], hid[at, :]
            sig = jax.nn.sigmoid(g)
            silu = g * sig
            h_ref[at, :] = (silu * u).astype(BF16)
            a_ref[at, :hidden] = (d * u * (sig * (1.0 + g * (1.0 - sig)))).astype(BF16)
            a_ref[at, hidden:] = (d * silu).astype(BF16)

    @pl.when(i >= steps)
    def _():
        ret_ref[...] = mm(a_ref[...], cat[part, :], NT).astype(BF16)


def weights_body(r_ref, g_ref, h_ref, a_ref, dg_ref, du_ref, dd_ref):
    width = r_ref.shape[1]
    hidden = h_ref.shape[1]
    chunk = 256

    @pl.loop(0, width // chunk)
    def _(c):
        cols = pl.ds(pl.multiple_of(c * chunk, chunk), chunk)
        both = mm(r_ref[:, cols], a_ref[...], TN)
        dg_ref[cols, :] = both[:, :hidden].astype(BF16)
        du_ref[cols, :] = both[:, hidden:].astype(BF16)
        dd_ref[:, cols] = mm(h_ref[...], g_ref[:, cols], TN).astype(BF16)


def combine_body(head, scaling, mt_ref, ret_ref, og_ref, q_ref, ag_ref, lg_ref):
    width = og_ref.shape[1]
    rows = ret_ref.shape[1]
    total = og_ref[...].astype(F32)
    for p in range(2):
        both = (ret_ref[2 * p].astype(F32) + ret_ref[2 * p + 1].astype(F32)).astype(BF16)
        total = total + mm(mt_ref[:, p * rows : (p + 1) * rows], both)
    grad = total.astype(BF16)
    ag_ref[...] = grad
    for h in range(width // head):
        cols = slice(h * head, (h + 1) * head)
        lg_ref[cols, :] = (scaling * mm(q_ref[:, cols], grad[:, cols], TN)).astype(BF16)


def back_query_body(head, scaling, mk_ref, v_ref, ag_ref, s_ref, gq_ref):
    length, width = mk_ref.shape
    t = lax.broadcasted_iota(jnp.int32, (length, length), 0)
    s = lax.broadcasted_iota(jnp.int32, (length, length), 1)
    for h in range(width // head):
        cols = slice(h * head, (h + 1) * head)
        ag = ag_ref[:, cols]
        back = jnp.where(t >= s, mm(ag, v_ref[:, cols], NT), 0.0).astype(BF16)
        total = mm(back, mk_ref[:, cols]) + mm(ag, s_ref[cols, :], NT)
        gq_ref[:, cols] = (scaling * total).astype(BF16)


def back_body(head, scaling, q_ref, mk_ref, v_ref, ag_ref, gk_ref, gv_ref):
    length, width = q_ref.shape
    s = lax.broadcasted_iota(jnp.int32, (length, length), 0)
    t = lax.broadcasted_iota(jnp.int32, (length, length), 1)
    for h in range(width // head):
        cols = slice(h * head, (h + 1) * head)
        q, ag = q_ref[:, cols], ag_ref[:, cols]
        back = jnp.where(t >= s, mm(v_ref[:, cols], ag, NT), 0.0).astype(BF16)
        gk_ref[:, cols] = scaling * mm(back, q)
        scores = jnp.where(t >= s, mm(mk_ref[:, cols], q, NT), 0.0).astype(BF16)
        gv_ref[:, cols] = scaling * mm(scores, ag)


def final_body(head, mk_ref, v_ref, s_ref, g_ref, gki_ref, gvi_ref, gk_ref, gv_ref):
    width = mk_ref.shape[1]
    gate = spike_columns(s_ref[...], pl.program_id(0), width, head)
    for h in range(width // head):
        cols = slice(h * head, (h + 1) * head)
        state = g_ref[cols, :]
        gk = gki_ref[:, cols] + mm(v_ref[:, cols], state, NT)
        gk_ref[:, cols] = (gate[:, cols] * gk).astype(BF16)
        gv_ref[:, cols] = (gvi_ref[:, cols] + mm(mk_ref[:, cols], state)).astype(BF16)


def shape(*dims, dtype=BF16):
    return jax.ShapeDtypeStruct(dims, dtype)


def on_device(
    queries,
    key_vectors,
    value_vectors,
    spikes,
    routes,
    route_probs,
    gate_weight,
    up_weight,
    down_weight,
    out_grad,
):
    length, width = queries.shape
    heads = spikes.shape[1]
    head = width // heads
    tokens, model = out_grad.shape
    top = routes.shape[1]
    ctx = lax.axis_size("ctx")
    exp = lax.axis_size("exp")
    devices = ctx * exp
    experts = devices // 2
    capacity = 2 * max(1, 3 * tokens * top // (4 * experts))
    scaling = 1.0 / math.sqrt(head * length * ctx)
    hidden = gate_weight.shape[2]
    slots = exp * capacity
    half_rows = ctx * slots
    rows = 2 * half_rows
    pair = 4 * head
    pairs = width // pair
    everywhere = ("exp", "ctx")

    def cols(n=1, m=1):
        return pl.BlockSpec((n, m), lambda i: (0, i))

    def whole(*dims):
        return pl.BlockSpec(dims, lambda i: (0,) * len(dims))

    tall = pl.BlockSpec((pair, head), lambda i: (i, 0))
    wide = cols(length, pair)
    seq = shape(length, width)
    seq32 = shape(length, width, dtype=F32)
    unit = length * width * 2
    spikes_t = spikes.T

    def exchange(part, reverse, cover):
        pieces = part.reshape(ctx, heads * head // ctx, head)
        pieces = lax.all_to_all(pieces, "ctx", 0, 0, tiled=True)
        pieces, cover = lax.optimization_barrier((pieces, cover))
        pieces = call(
            functools.partial(sum_body, reverse), (1,),
            [whole(*pieces.shape)], whole(*pieces.shape), shape(*pieces.shape), 1e6, 1 << 19, 4,
        )(pieces)
        pieces = lax.all_to_all(pieces, "ctx", 0, 0, tiled=True)
        return pieces.reshape(heads * head, head), cover

    block_state, masked = call(
        functools.partial(state_body, head), (pairs,),
        [wide, wide, whole(heads, length)], [tall, wide],
        [shape(heads * head, head), seq], 2 * length * width * head, 3 * unit,
    )(key_vectors, value_vectors, spikes_t)
    mine = lax.axis_index("exp").reshape(1)
    smem = pl.BlockSpec(memory_space=pltpu.SMEM)
    piece = (tokens + 16, width)
    own_grad, block_state = lax.optimization_barrier((out_grad, block_state))
    pieces = call(
        functools.partial(cut_body, capacity, slots, half_rows), (1,),
        [smem, whole(tokens, model), whole(top, tokens), whole(top, tokens)],
        [whole(*piece)] * exp, [shape(*piece)] * exp, 1e6, 2 * unit,
    )(mine, own_grad, routes.T, route_probs.T)
    pieces = [pieces[0]] + [
        lax.ppermute(pieces[i], "exp", [(j, (j + i) % exp) for j in range(exp)])
        for i in range(1, exp)
    ]
    states_in, _ = exchange(block_state, False, ())
    send_shape = shape(2, 2, half_rows, 2 * width)
    send_flops = 2 * rows * length * width
    send_bytes = 4 * rows * width + 2 * rows * length + 2 * unit
    grad_cols, select, buffer = call(
        functools.partial(prepare_body, exp), (1 + pairs,), [smem] + [whole(*piece)] * exp,
        [
            whole(length, width), whole(rows, length),
            pl.BlockSpec(
                (2, 2, half_rows, pair), lambda i: (0, 0, 0, jnp.maximum(i - 1, 0) + pairs)
            ),
        ],
        [seq, shape(rows, length), send_shape], send_flops, send_bytes,
        scratch_shapes=[pltpu.VMEM((rows, length), BF16)],
    )(mine, *pieces)
    buffer = call(
        functools.partial(rows_body, head, scaling), (pairs,),
        [whole(rows, length), wide, wide, wide, tall, pl.BlockSpec(memory_space=pl.ANY)],
        pl.BlockSpec((2, 2, half_rows, pair), lambda i: (0, 0, 0, i)),
        send_shape, send_flops, send_bytes, 52, input_output_aliases={5: 0},
    )(select, queries, masked, value_vectors, states_in, buffer)
    got = lax.all_to_all(
        buffer.reshape(devices, slots, 2 * width), everywhere, 0, 0, tiled=True
    ).reshape(exp * half_rows, 2 * width)

    act = shape(half_rows, hidden)
    last = exp - 1
    block = half_rows * width * 2
    back_rows, hid, acts = call(
        functools.partial(expert_body, exp), (2 * exp,),
        [
            pl.BlockSpec((half_rows, width), lambda i: (jnp.minimum(i, last), 0)),
            pl.BlockSpec((half_rows, width), lambda i: (jnp.minimum(i, last), 1)),
            pl.BlockSpec((width, hidden), lambda i: (jnp.minimum(i, last), 0)),
            pl.BlockSpec((width, hidden), lambda i: (jnp.minimum(i, last), 0)),
            pl.BlockSpec((hidden, width), lambda i: (0, jnp.minimum(i, last))),
        ],
        [
            pl.BlockSpec((half_rows, width), lambda i: (jnp.maximum(i - exp, 0), 0)),
            whole(half_rows, hidden),
            whole(half_rows, 2 * hidden),
        ],
        [shape(exp * half_rows, width), act, shape(half_rows, 2 * hidden)],
        10 * half_rows * model * hidden, 12 * block + 10 * model * hidden,
        scratch_shapes=[
            pltpu.VMEM((half_rows, 2 * hidden), F32), pltpu.VMEM((half_rows, hidden), F32),
            pltpu.VMEM((model, 2 * hidden), BF16),
        ],
    )(got, got, gate_weight[0], up_weight[0], down_weight[0])
    returned = lax.all_to_all(
        back_rows.reshape(devices, slots, width), everywhere, 0, 0, tiled=True
    ).reshape(exp, half_rows, width)
    grad_gate, grad_up, grad_down = call(
        weights_body, (exp,),
        [
            pl.BlockSpec((half_rows, width), lambda i: (i, 0)),
            pl.BlockSpec((half_rows, width), lambda i: (i, 1)),
            whole(half_rows, hidden),
            whole(half_rows, 2 * hidden),
        ],
        [
            pl.BlockSpec((width, hidden), lambda i: (i, 0)),
            pl.BlockSpec((width, hidden), lambda i: (i, 0)),
            pl.BlockSpec((hidden, width), lambda i: (0, i)),
        ],
        [shape(model, hidden), shape(model, hidden), shape(hidden, model)],
        6 * half_rows * model * hidden, 8 * block + 6 * model * hidden,
    )(got, got, hid, acts)

    far_pieces, acts = lax.optimization_barrier((tuple(pieces), acts))
    select_t = call(
        functools.partial(select_t_body, exp), (1,), [smem] + [whole(*piece)] * exp,
        whole(length, rows), shape(length, rows), 1e6, 2 * rows * length + unit,
    )(mine, *far_pieces)
    returned, select_t, grad_gate, grad_up, grad_down = lax.optimization_barrier(
        (returned, select_t, grad_gate, grad_up, grad_down)
    )

    att_grad, local_grad = call(
        functools.partial(combine_body, head, scaling), (pairs,),
        [whole(length, rows), pl.BlockSpec((exp, half_rows, pair), lambda i: (0, 0, i)), wide, wide],
        [wide, tall], [seq, shape(heads * head, head)],
        2 * rows * length * width, 2 * rows * length + 4 * block + 3 * unit,
    )(select_t, returned, grad_cols, queries)
    parts = call(
        functools.partial(back_body, head, scaling), (pairs,), [wide] * 4, [wide] * 2,
        [seq32, seq32], 8 * length * length * width, 8 * unit,
    )(queries, masked, value_vectors, att_grad)
    grad_states, (keys_part, values_part) = exchange(local_grad, True, tuple(parts))
    grad_queries = call(
        functools.partial(back_query_body, head, scaling), (pairs,), [wide] * 3 + [tall], wide, seq,
        4 * length * length * width, 4 * unit,
    )(masked, value_vectors, att_grad, states_in)
    grad_keys, grad_values = call(
        functools.partial(final_body, head), (pairs,),
        [wide, wide, whole(heads, length), tall, wide, wide], [wide] * 2, [seq, seq],
        4 * length * width * head, 8 * unit, 52,
    )(masked, value_vectors, spikes_t, grad_states, keys_part, values_part)
    return grad_queries, grad_keys, grad_values, grad_gate[None], grad_up[None], grad_down[None]


def solution(mesh):
    by_head = P("ctx", "exp")
    by_device = P(("ctx", "exp"), None)
    by_half = P(("ctx", "exp"), None, None)
    return jax.shard_map(
        on_device,
        mesh=mesh,
        in_specs=(by_head,) * 4 + (by_device,) * 2 + (by_half,) * 3 + (by_device,),
        out_specs=(by_head,) * 3 + (by_half,) * 3,
        check_vma=False,
    )
```

```python
import functools
import math

import jax
import jax.numpy as jnp
from jax import lax
from jax.experimental import pallas as pl
from jax.experimental.pallas import tpu as pltpu
from jax.sharding import PartitionSpec as P

F32 = jnp.float32
BF16 = jnp.bfloat16
NN = (((1,), (0,)), ((), ()))
NT = (((1,), (1,)), ((), ()))
TN = (((0,), (0,)), ((), ()))


def mm(a, b, dims=NN):
    return lax.dot_general(a, b, dims, preferred_element_type=F32)


def call(body, grid, in_specs, out_specs, out_shape, flops, nbytes, vmem=60, **kw):
    return pl.pallas_call(
        body,
        grid=grid,
        in_specs=in_specs,
        out_specs=out_specs,
        out_shape=out_shape,
        compiler_params=pltpu.CompilerParams(
            dimension_semantics=("arbitrary",) * len(grid), vmem_limit_bytes=vmem << 20
        ),
        cost_estimate=pl.CostEstimate(
            flops=int(flops), bytes_accessed=int(nbytes), transcendentals=0
        ),
        **kw,
    )


def spike_columns(spikes, pair, width, head):
    heads = spikes.shape[0]
    col = lax.broadcasted_iota(jnp.int32, (heads, width), 1) // head + pair * (width // head)
    row = lax.broadcasted_iota(jnp.int32, (heads, width), 0)
    spread = jnp.where(col == row, 1.0, 0.0).astype(BF16)
    return mm(spikes.astype(F32).astype(BF16), spread, TN)


def cut_body(capacity, slots, half_rows, mine_ref, x_ref, r_ref, p_ref, *o_refs):
    width = o_refs[0].shape[1]
    tokens = x_ref.shape[0]
    extra = o_refs[0].shape[0] - tokens
    row = lax.broadcasted_iota(jnp.int32, (tokens, tokens), 0)
    col = lax.broadcasted_iota(jnp.int32, (tokens, tokens), 1)

    def column(lanes):
        return jnp.sum(jnp.where(row == col, lanes, 0.0), axis=1, keepdims=True)

    named = r_ref[...].astype(F32)
    probs = p_ref[...].astype(F32)
    line = lax.broadcasted_iota(jnp.int32, (extra, tokens), 0)
    pack = jnp.zeros((extra, tokens), F32)
    first, second = column(named[0:1, :]), column(named[1:2, :])
    for k in range(2):
        expert = named[k : k + 1, :]
        same = jnp.where(first == expert, 1.0, 0.0) + jnp.where(second == expert, 1.0, 0.0)
        slot = jnp.sum(jnp.where(row < col, same, 0.0), axis=0, keepdims=True)
        half = jnp.floor(expert * 0.5)
        place = (expert - 2.0 * half) * half_rows + half * slots + slot
        place = place + (mine_ref[0] * capacity).astype(F32)
        high = jnp.floor(place * 0.125)
        for at, value in (
            (3 * k, high), (3 * k + 1, place - 8.0 * high), (3 * k + 2, probs[k : k + 1, :])
        ):
            pack = jnp.where(line == at, value, pack)
    for i, o_ref in enumerate(o_refs):
        at = lax.rem(mine_ref[0] + i, len(o_refs)) * width
        o_ref[:tokens, :] = x_ref[:, pl.ds(pl.multiple_of(at, width), width)]
        o_ref[tokens:, :] = jnp.zeros((extra, width), BF16)
        o_ref[tokens:, :tokens] = pack.astype(BF16)


def prepare_body(count, mine_ref, *refs):
    x_refs, (g_ref, m_ref, o_ref, w_ref) = refs[:count], refs[count:]
    rows = m_ref.shape[0]
    tokens = g_ref.shape[0] // count
    pair = o_ref.shape[3]
    step = pl.program_id(0)

    @pl.when(step == 0)
    def _():
        down = lax.broadcasted_iota(jnp.int32, (rows, tokens), 0).astype(F32)
        for i, x_ref in enumerate(x_refs):
            at = pl.multiple_of(lax.rem(mine_ref[0] + count - i, count) * tokens, tokens)
            g_ref[pl.ds(at, tokens), :] = x_ref[:tokens, :]
            pack = x_ref[tokens:, :tokens].astype(F32)
            first = 8.0 * pack[0:1] + pack[1:2]
            second = 8.0 * pack[3:4] + pack[4:5]
            hit0, hit1 = down == first, down == second
            m_ref[:, pl.ds(at, tokens)] = jnp.where(hit0 | hit1, 1.0, 0.0).astype(BF16)
            w_ref[:, pl.ds(at, tokens)] = jnp.where(
                hit0, pack[2:3], jnp.where(hit1, pack[5:6], 0.0)
            ).astype(BF16)

    cols = pl.ds(pl.multiple_of(step * pair, pair), pair)
    put_rows(w_ref, g_ref[:, cols], o_ref)


def state_body(head, k_ref, v_ref, s_ref, bs_ref, mk_ref):
    width = k_ref.shape[1]
    gate = spike_columns(s_ref[...], pl.program_id(0), width, head)
    masked = (k_ref[...].astype(F32) * gate).astype(BF16)
    mk_ref[...] = masked
    value = v_ref[...]
    for h in range(width // head):
        cols = slice(h * head, (h + 1) * head)
        bs_ref[cols, :] = mm(masked[:, cols], value[:, cols], TN).astype(BF16)


def intra_body(head, q_ref, mk_ref, v_ref, o_ref):
    length, width = q_ref.shape
    t = lax.broadcasted_iota(jnp.int32, (length, length), 0)
    s = lax.broadcasted_iota(jnp.int32, (length, length), 1)
    for h in range(width // head):
        cols = slice(h * head, (h + 1) * head)
        scores = mm(q_ref[:, cols], mk_ref[:, cols], NT)
        scores = jnp.where(t >= s, scores, 0.0).astype(BF16)
        o_ref[:, cols] = mm(scores, v_ref[:, cols])


def sum_body(reverse, x_ref, o_ref):
    count = x_ref.shape[0]

    def step(i, total):
        at = count - 1 - i if reverse else i
        o_ref[at] = total.astype(BF16)
        return total + x_ref[at].astype(F32)

    lax.fori_loop(0, count, step, jnp.zeros(x_ref.shape[1:], F32), unroll=True)


def select_t_body(count, mine_ref, *refs):
    x_refs, mt_ref = refs[:count], refs[count]
    rows = mt_ref.shape[1]
    tokens = mt_ref.shape[0] // count
    across = lax.broadcasted_iota(jnp.int32, (tokens, rows), 1).astype(F32)
    eye = lax.broadcasted_iota(jnp.int32, (tokens, tokens), 0) == lax.broadcasted_iota(
        jnp.int32, (tokens, tokens), 1
    )
    for i, x_ref in enumerate(x_refs):
        at = pl.multiple_of(lax.rem(mine_ref[0] + count - i, count) * tokens, tokens)
        pack = x_ref[tokens:, :tokens].astype(F32)
        first, second = 8.0 * pack[0:1] + pack[1:2], 8.0 * pack[3:4] + pack[4:5]
        first = jnp.sum(jnp.where(eye, first, 0.0), axis=1, keepdims=True)
        second = jnp.sum(jnp.where(eye, second, 0.0), axis=1, keepdims=True)
        mt_ref[pl.ds(at, tokens), :] = jnp.where(
            (across == first) | (across == second), 1.0, 0.0
        ).astype(BF16)


def put_rows(m_ref, columns, o_ref):
    rows = o_ref.shape[2]
    for p in range(2):
        picked = mm(m_ref[p * rows : (p + 1) * rows, :], columns).astype(BF16)
        o_ref[p, 0] = picked
        o_ref[p, 1] = picked


def rows_body(head, scaling, m_ref, q_ref, intra_ref, s_ref, buf_ref, o_ref):
    del buf_ref
    width = q_ref.shape[1]
    parts = []
    for h in range(width // head):
        cols = slice(h * head, (h + 1) * head)
        total = intra_ref[:, cols] + mm(q_ref[:, cols], s_ref[cols, :])
        parts.append((scaling * total).astype(BF16))
    put_rows(m_ref, jnp.concatenate(parts, axis=1), o_ref)


def expert_body(
    steps, r_ref, g_ref, wg_ref, wu_ref, wd_ref, ret_ref, h_ref, a_ref, both, hid, cat
):
    i = pl.program_id(0)
    rows, hidden = hid.shape
    width = r_ref.shape[1]
    chunk = rows // 3
    part = pl.ds(pl.multiple_of(lax.rem(i, steps) * width, width), width)

    @pl.when(i < steps)
    def _():
        cat[part, :hidden] = wg_ref[...]
        cat[part, hidden:] = wu_ref[...]

    @pl.when(i == 0)
    def _():
        both[...] = mm(r_ref[...], cat[part, :])
        hid[...] = mm(g_ref[...], wd_ref[...], NT)

    @pl.when((i > 0) & (i < steps - 1))
    def _():
        both[...] += mm(r_ref[...], cat[part, :])
        hid[...] += mm(g_ref[...], wd_ref[...], NT)

    @pl.when(i == steps - 1)
    def _():
        for c in range(rows // chunk):
            at = slice(c * chunk, (c + 1) * chunk)
            total = both[at, :] + mm(r_ref[at, :], cat[part, :])
            d = hid[at, :] + mm(g_ref[at, :], wd_ref[...], NT)
            g, u = total[:, :hidden], total[:, hidden:]
            sig = jax.nn.sigmoid(g)
            silu = g * sig
            h_ref[at, :] = (silu * u).astype(BF16)
            a_ref[at, :hidden] = (d * u * (sig * (1.0 + g * (1.0 - sig)))).astype(BF16)
            a_ref[at, hidden:] = (d * silu).astype(BF16)

    @pl.when(i >= steps)
    def _():
        ret_ref[...] = mm(a_ref[...], cat[part, :], NT).astype(BF16)


def weights_body(r_ref, g_ref, h_ref, a_ref, dg_ref, du_ref, dd_ref):
    width = r_ref.shape[1]
    hidden = h_ref.shape[1]
    chunk = 256

    @pl.loop(0, width // chunk)
    def _(c):
        cols = pl.ds(pl.multiple_of(c * chunk, chunk), chunk)
        both = mm(r_ref[:, cols], a_ref[...], TN)
        dg_ref[cols, :] = both[:, :hidden].astype(BF16)
        du_ref[cols, :] = both[:, hidden:].astype(BF16)
        dd_ref[:, cols] = mm(h_ref[...], g_ref[:, cols], TN).astype(BF16)


def combine_body(head, scaling, mt_ref, ret_ref, og_ref, q_ref, ag_ref, lg_ref):
    width = og_ref.shape[1]
    rows = ret_ref.shape[1]
    total = og_ref[...].astype(F32)
    for p in range(2):
        both = (ret_ref[2 * p].astype(F32) + ret_ref[2 * p + 1].astype(F32)).astype(BF16)
        total = total + mm(mt_ref[:, p * rows : (p + 1) * rows], both)
    grad = total.astype(BF16)
    ag_ref[...] = grad
    for h in range(width // head):
        cols = slice(h * head, (h + 1) * head)
        lg_ref[cols, :] = (scaling * mm(q_ref[:, cols], grad[:, cols], TN)).astype(BF16)


def back_query_body(head, scaling, mk_ref, v_ref, ag_ref, s_ref, gq_ref):
    length, width = mk_ref.shape
    t = lax.broadcasted_iota(jnp.int32, (length, length), 0)
    s = lax.broadcasted_iota(jnp.int32, (length, length), 1)
    for h in range(width // head):
        cols = slice(h * head, (h + 1) * head)
        ag = ag_ref[:, cols]
        back = jnp.where(t >= s, mm(ag, v_ref[:, cols], NT), 0.0).astype(BF16)
        total = mm(back, mk_ref[:, cols]) + mm(ag, s_ref[cols, :], NT)
        gq_ref[:, cols] = (scaling * total).astype(BF16)


def back_body(head, scaling, q_ref, mk_ref, v_ref, ag_ref, gk_ref, gv_ref):
    length, width = q_ref.shape
    s = lax.broadcasted_iota(jnp.int32, (length, length), 0)
    t = lax.broadcasted_iota(jnp.int32, (length, length), 1)
    for h in range(width // head):
        cols = slice(h * head, (h + 1) * head)
        q, ag = q_ref[:, cols], ag_ref[:, cols]
        back = jnp.where(t >= s, mm(v_ref[:, cols], ag, NT), 0.0).astype(BF16)
        gk_ref[:, cols] = scaling * mm(back, q)
        scores = jnp.where(t >= s, mm(mk_ref[:, cols], q, NT), 0.0).astype(BF16)
        gv_ref[:, cols] = scaling * mm(scores, ag)


def final_body(head, mk_ref, v_ref, s_ref, g_ref, gki_ref, gvi_ref, gk_ref, gv_ref):
    width = mk_ref.shape[1]
    gate = spike_columns(s_ref[...], pl.program_id(0), width, head)
    for h in range(width // head):
        cols = slice(h * head, (h + 1) * head)
        state = g_ref[cols, :]
        gk = gki_ref[:, cols] + mm(v_ref[:, cols], state, NT)
        gk_ref[:, cols] = (gate[:, cols] * gk).astype(BF16)
        gv_ref[:, cols] = (gvi_ref[:, cols] + mm(mk_ref[:, cols], state)).astype(BF16)


def shape(*dims, dtype=BF16):
    return jax.ShapeDtypeStruct(dims, dtype)


def on_device(
    queries,
    key_vectors,
    value_vectors,
    spikes,
    routes,
    route_probs,
    gate_weight,
    up_weight,
    down_weight,
    out_grad,
):
    length, width = queries.shape
    heads = spikes.shape[1]
    head = width // heads
    tokens, model = out_grad.shape
    top = routes.shape[1]
    ctx = lax.axis_size("ctx")
    exp = lax.axis_size("exp")
    devices = ctx * exp
    experts = devices // 2
    capacity = 2 * max(1, 3 * tokens * top // (4 * experts))
    scaling = 1.0 / math.sqrt(head * length * ctx)
    hidden = gate_weight.shape[2]
    slots = exp * capacity
    half_rows = ctx * slots
    rows = 2 * half_rows
    pair = 4 * head
    pairs = width // pair
    everywhere = ("exp", "ctx")

    def cols(n=1, m=1):
        return pl.BlockSpec((n, m), lambda i: (0, i))

    def whole(*dims):
        return pl.BlockSpec(dims, lambda i: (0,) * len(dims))

    tall = pl.BlockSpec((pair, head), lambda i: (i, 0))
    wide = cols(length, pair)
    seq = shape(length, width)
    seq32 = shape(length, width, dtype=F32)
    unit = length * width * 2
    spikes_t = spikes.T

    def exchange(part, reverse, cover):
        pieces = part.reshape(ctx, heads * head // ctx, head)
        pieces = lax.all_to_all(pieces, "ctx", 0, 0, tiled=True)
        pieces, cover = lax.optimization_barrier((pieces, cover))
        pieces = call(
            functools.partial(sum_body, reverse), (1,),
            [whole(*pieces.shape)], whole(*pieces.shape), shape(*pieces.shape), 1e6, 1 << 19, 4,
        )(pieces)
        pieces = lax.all_to_all(pieces, "ctx", 0, 0, tiled=True)
        return pieces.reshape(heads * head, head), cover

    block_state, masked = call(
        functools.partial(state_body, head), (pairs,),
        [wide, wide, whole(heads, length)], [tall, wide],
        [shape(heads * head, head), seq], 2 * length * width * head, 3 * unit,
    )(key_vectors, value_vectors, spikes_t)
    mine = lax.axis_index("exp").reshape(1)
    smem = pl.BlockSpec(memory_space=pltpu.SMEM)
    piece = (tokens + 16, width)
    own_grad, block_state = lax.optimization_barrier((out_grad, block_state))
    pieces = call(
        functools.partial(cut_body, capacity, slots, half_rows), (1,),
        [smem, whole(tokens, model), whole(top, tokens), whole(top, tokens)],
        [whole(*piece)] * exp, [shape(*piece)] * exp, 1e6, 2 * unit,
    )(mine, own_grad, routes.T, route_probs.T)
    pieces = list(pieces)
    for i in sorted(range(1, exp), key=lambda i: -min(i, exp - i)):
        pieces[i] = lax.ppermute(pieces[i], "exp", [(j, (j + i) % exp) for j in range(exp)])
    states_in, _ = exchange(block_state, False, ())
    intra = call(
        functools.partial(intra_body, head), (pairs,), [wide] * 3, wide, seq32,
        4 * length * length * width, 5 * unit,
    )(queries, masked, value_vectors)

    send_shape = shape(2, 2, half_rows, 2 * width)
    send_flops = 2 * rows * length * width
    send_bytes = 4 * rows * width + 2 * rows * length + 2 * unit
    grad_cols, select, buffer = call(
        functools.partial(prepare_body, exp), (pairs,), [smem] + [whole(*piece)] * exp,
        [
            whole(length, width), whole(rows, length),
            pl.BlockSpec((2, 2, half_rows, pair), lambda i: (0, 0, 0, i + pairs)),
        ],
        [seq, shape(rows, length), send_shape], send_flops, send_bytes,
        scratch_shapes=[pltpu.VMEM((rows, length), BF16)],
    )(mine, *pieces)
    buffer = call(
        functools.partial(rows_body, head, scaling), (pairs,),
        [whole(rows, length), wide, wide, tall, pl.BlockSpec(memory_space=pl.ANY)],
        pl.BlockSpec((2, 2, half_rows, pair), lambda i: (0, 0, 0, i)),
        send_shape, send_flops, send_bytes, 52, input_output_aliases={4: 0},
    )(select, queries, intra, states_in, buffer)
    got = lax.all_to_all(
        buffer.reshape(devices, slots, 2 * width), everywhere, 0, 0, tiled=True
    ).reshape(exp * half_rows, 2 * width)

    act = shape(half_rows, hidden)
    last = exp - 1
    block = half_rows * width * 2
    back_rows, hid, acts = call(
        functools.partial(expert_body, exp), (2 * exp,),
        [
            pl.BlockSpec((half_rows, width), lambda i: (jnp.minimum(i, last), 0)),
            pl.BlockSpec((half_rows, width), lambda i: (jnp.minimum(i, last), 1)),
            pl.BlockSpec((width, hidden), lambda i: (jnp.minimum(i, last), 0)),
            pl.BlockSpec((width, hidden), lambda i: (jnp.minimum(i, last), 0)),
            pl.BlockSpec((hidden, width), lambda i: (0, jnp.minimum(i, last))),
        ],
        [
            pl.BlockSpec((half_rows, width), lambda i: (jnp.maximum(i - exp, 0), 0)),
            whole(half_rows, hidden),
            whole(half_rows, 2 * hidden),
        ],
        [shape(exp * half_rows, width), act, shape(half_rows, 2 * hidden)],
        10 * half_rows * model * hidden, 12 * block + 10 * model * hidden,
        scratch_shapes=[
            pltpu.VMEM((half_rows, 2 * hidden), F32), pltpu.VMEM((half_rows, hidden), F32),
            pltpu.VMEM((model, 2 * hidden), BF16),
        ],
    )(got, got, gate_weight[0], up_weight[0], down_weight[0])
    returned = lax.all_to_all(
        back_rows.reshape(devices, slots, width), everywhere, 0, 0, tiled=True
    ).reshape(exp, half_rows, width)
    grad_gate, grad_up, grad_down = call(
        weights_body, (exp,),
        [
            pl.BlockSpec((half_rows, width), lambda i: (i, 0)),
            pl.BlockSpec((half_rows, width), lambda i: (i, 1)),
            whole(half_rows, hidden),
            whole(half_rows, 2 * hidden),
        ],
        [
            pl.BlockSpec((width, hidden), lambda i: (i, 0)),
            pl.BlockSpec((width, hidden), lambda i: (i, 0)),
            pl.BlockSpec((hidden, width), lambda i: (0, i)),
        ],
        [shape(model, hidden), shape(model, hidden), shape(hidden, model)],
        6 * half_rows * model * hidden, 8 * block + 6 * model * hidden,
    )(got, got, hid, acts)

    far_pieces, acts = lax.optimization_barrier((tuple(pieces), acts))
    select_t = call(
        functools.partial(select_t_body, exp), (1,), [smem] + [whole(*piece)] * exp,
        whole(length, rows), shape(length, rows), 1e6, 2 * rows * length + unit,
    )(mine, *far_pieces)
    returned, select_t, grad_gate, grad_up, grad_down = lax.optimization_barrier(
        (returned, select_t, grad_gate, grad_up, grad_down)
    )

    att_grad, local_grad = call(
        functools.partial(combine_body, head, scaling), (pairs,),
        [whole(length, rows), pl.BlockSpec((exp, half_rows, pair), lambda i: (0, 0, i)), wide, wide],
        [wide, tall], [seq, shape(heads * head, head)],
        2 * rows * length * width, 2 * rows * length + 4 * block + 3 * unit,
    )(select_t, returned, grad_cols, queries)
    parts = call(
        functools.partial(back_body, head, scaling), (pairs,), [wide] * 4, [wide] * 2,
        [seq32, seq32], 8 * length * length * width, 8 * unit,
    )(queries, masked, value_vectors, att_grad)
    grad_states, (keys_part, values_part) = exchange(local_grad, True, tuple(parts))
    grad_queries = call(
        functools.partial(back_query_body, head, scaling), (pairs,), [wide] * 3 + [tall], wide, seq,
        4 * length * length * width, 4 * unit,
    )(masked, value_vectors, att_grad, states_in)
    grad_keys, grad_values = call(
        functools.partial(final_body, head), (pairs,),
        [wide, wide, whole(heads, length), tall, wide, wide], [wide] * 2, [seq, seq],
        4 * length * width * head, 8 * unit, 52,
    )(masked, value_vectors, spikes_t, grad_states, keys_part, values_part)
    return grad_queries, grad_keys, grad_values, grad_gate[None], grad_up[None], grad_down[None]


def solution(mesh):
    by_head = P("ctx", "exp")
    by_device = P(("ctx", "exp"), None)
    by_half = P(("ctx", "exp"), None, None)
    return jax.shard_map(
        on_device,
        mesh=mesh,
        in_specs=(by_head,) * 4 + (by_device,) * 2 + (by_half,) * 3 + (by_device,),
        out_specs=(by_head,) * 3 + (by_half,) * 3,
        check_vma=False,
    )
```

```python
import functools
import math

import jax
import jax.numpy as jnp
from jax import lax
from jax.experimental import pallas as pl
from jax.experimental.pallas import tpu as pltpu
from jax.sharding import PartitionSpec as P

F32 = jnp.float32
BF16 = jnp.bfloat16
NN = (((1,), (0,)), ((), ()))
NT = (((1,), (1,)), ((), ()))
TN = (((0,), (0,)), ((), ()))


def mm(a, b, dims=NN):
    return lax.dot_general(a, b, dims, preferred_element_type=F32)


def call(body, grid, in_specs, out_specs, out_shape, flops, nbytes, vmem=60, **kw):
    return pl.pallas_call(
        body,
        grid=grid,
        in_specs=in_specs,
        out_specs=out_specs,
        out_shape=out_shape,
        compiler_params=pltpu.CompilerParams(
            dimension_semantics=("arbitrary",) * len(grid), vmem_limit_bytes=vmem << 20
        ),
        cost_estimate=pl.CostEstimate(
            flops=int(flops), bytes_accessed=int(nbytes), transcendentals=0
        ),
        **kw,
    )


def spike_columns(spikes, pair, width, head):
    heads = spikes.shape[0]
    col = lax.broadcasted_iota(jnp.int32, (heads, width), 1) // head + pair * (width // head)
    row = lax.broadcasted_iota(jnp.int32, (heads, width), 0)
    spread = jnp.where(col == row, 1.0, 0.0).astype(BF16)
    return mm(spikes.astype(F32).astype(BF16), spread, TN)


def cut_body(capacity, slots, half_rows, mine_ref, x_ref, r_ref, p_ref, *o_refs):
    width = o_refs[0].shape[1]
    tokens = x_ref.shape[0]
    extra = o_refs[0].shape[0] - tokens
    row = lax.broadcasted_iota(jnp.int32, (tokens, tokens), 0)
    col = lax.broadcasted_iota(jnp.int32, (tokens, tokens), 1)

    def column(lanes):
        return jnp.sum(jnp.where(row == col, lanes, 0.0), axis=1, keepdims=True)

    named = r_ref[...].astype(F32)
    probs = p_ref[...].astype(F32)
    line = lax.broadcasted_iota(jnp.int32, (extra, tokens), 0)
    pack = jnp.zeros((extra, tokens), F32)
    first, second = column(named[0:1, :]), column(named[1:2, :])
    for k in range(2):
        expert = named[k : k + 1, :]
        same = jnp.where(first == expert, 1.0, 0.0) + jnp.where(second == expert, 1.0, 0.0)
        slot = jnp.sum(jnp.where(row < col, same, 0.0), axis=0, keepdims=True)
        half = jnp.floor(expert * 0.5)
        place = (expert - 2.0 * half) * half_rows + half * slots + slot
        place = place + (mine_ref[0] * capacity).astype(F32)
        high = jnp.floor(place * 0.125)
        for at, value in (
            (3 * k, high), (3 * k + 1, place - 8.0 * high), (3 * k + 2, probs[k : k + 1, :])
        ):
            pack = jnp.where(line == at, value, pack)
    for i, o_ref in enumerate(o_refs):
        at = lax.rem(mine_ref[0] + i, len(o_refs)) * width
        o_ref[:tokens, :] = x_ref[:, pl.ds(pl.multiple_of(at, width), width)]
        o_ref[tokens:, :] = jnp.zeros((extra, width), BF16)
        o_ref[tokens:, :tokens] = pack.astype(BF16)


def prepare_body(count, mine_ref, *refs):
    x_refs, (g_ref, m_ref, o_ref, w_ref) = refs[:count], refs[count:]
    rows = m_ref.shape[0]
    tokens = g_ref.shape[0] // count
    pair = o_ref.shape[3]
    step = pl.program_id(0)

    @pl.when(step == 0)
    def _():
        down = lax.broadcasted_iota(jnp.int32, (rows, tokens), 0).astype(F32)
        for i, x_ref in enumerate(x_refs):
            at = pl.multiple_of(lax.rem(mine_ref[0] + count - i, count) * tokens, tokens)
            g_ref[pl.ds(at, tokens), :] = x_ref[:tokens, :]
            pack = x_ref[tokens:, :tokens].astype(F32)
            first = 8.0 * pack[0:1] + pack[1:2]
            second = 8.0 * pack[3:4] + pack[4:5]
            hit0, hit1 = down == first, down == second
            m_ref[:, pl.ds(at, tokens)] = jnp.where(hit0 | hit1, 1.0, 0.0).astype(BF16)
            w_ref[:, pl.ds(at, tokens)] = jnp.where(
                hit0, pack[2:3], jnp.where(hit1, pack[5:6], 0.0)
            ).astype(BF16)

    cols = pl.ds(pl.multiple_of(step * pair, pair), pair)
    put_rows(w_ref, g_ref[:, cols], o_ref)


def state_body(head, k_ref, v_ref, s_ref, bs_ref, mk_ref):
    width = k_ref.shape[1]
    gate = spike_columns(s_ref[...], pl.program_id(0), width, head)
    masked = (k_ref[...].astype(F32) * gate).astype(BF16)
    mk_ref[...] = masked
    value = v_ref[...]
    for h in range(width // head):
        cols = slice(h * head, (h + 1) * head)
        bs_ref[cols, :] = mm(masked[:, cols], value[:, cols], TN).astype(BF16)


def intra_body(head, q_ref, mk_ref, v_ref, o_ref):
    length, width = q_ref.shape
    t = lax.broadcasted_iota(jnp.int32, (length, length), 0)
    s = lax.broadcasted_iota(jnp.int32, (length, length), 1)
    for h in range(width // head):
        cols = slice(h * head, (h + 1) * head)
        scores = mm(q_ref[:, cols], mk_ref[:, cols], NT)
        scores = jnp.where(t >= s, scores, 0.0).astype(BF16)
        o_ref[:, cols] = mm(scores, v_ref[:, cols]).astype(BF16)


def sum_body(reverse, x_ref, o_ref):
    count = x_ref.shape[0]

    def step(i, total):
        at = count - 1 - i if reverse else i
        o_ref[at] = total.astype(BF16)
        return total + x_ref[at].astype(F32)

    lax.fori_loop(0, count, step, jnp.zeros(x_ref.shape[1:], F32), unroll=True)


def select_t_body(count, mine_ref, *refs):
    x_refs, mt_ref = refs[:count], refs[count]
    rows = mt_ref.shape[1]
    tokens = mt_ref.shape[0] // count
    across = lax.broadcasted_iota(jnp.int32, (tokens, rows), 1).astype(F32)
    eye = lax.broadcasted_iota(jnp.int32, (tokens, tokens), 0) == lax.broadcasted_iota(
        jnp.int32, (tokens, tokens), 1
    )
    for i, x_ref in enumerate(x_refs):
        at = pl.multiple_of(lax.rem(mine_ref[0] + count - i, count) * tokens, tokens)
        pack = x_ref[tokens:, :tokens].astype(F32)
        first, second = 8.0 * pack[0:1] + pack[1:2], 8.0 * pack[3:4] + pack[4:5]
        first = jnp.sum(jnp.where(eye, first, 0.0), axis=1, keepdims=True)
        second = jnp.sum(jnp.where(eye, second, 0.0), axis=1, keepdims=True)
        mt_ref[pl.ds(at, tokens), :] = jnp.where(
            (across == first) | (across == second), 1.0, 0.0
        ).astype(BF16)


def put_rows(m_ref, columns, o_ref):
    rows = o_ref.shape[2]
    for p in range(2):
        picked = mm(m_ref[p * rows : (p + 1) * rows, :], columns).astype(BF16)
        o_ref[p, 0] = picked
        o_ref[p, 1] = picked


def rows_body(head, scaling, m_ref, q_ref, intra_ref, s_ref, buf_ref, o_ref):
    del buf_ref
    width = q_ref.shape[1]
    parts = []
    for h in range(width // head):
        cols = slice(h * head, (h + 1) * head)
        total = intra_ref[:, cols].astype(F32) + mm(q_ref[:, cols], s_ref[cols, :])
        parts.append((scaling * total).astype(BF16))
    put_rows(m_ref, jnp.concatenate(parts, axis=1), o_ref)


def expert_body(
    steps, r_ref, g_ref, wg_ref, wu_ref, wd_ref, ret_ref, h_ref, a_ref, both, hid, cat
):
    i = pl.program_id(0)
    rows, hidden = hid.shape
    width = r_ref.shape[1]
    chunk = rows // 3
    part = pl.ds(pl.multiple_of(lax.rem(i, steps) * width, width), width)

    @pl.when(i < steps)
    def _():
        cat[part, :hidden] = wg_ref[...]
        cat[part, hidden:] = wu_ref[...]

    @pl.when(i == 0)
    def _():
        both[...] = mm(r_ref[...], cat[part, :])
        hid[...] = mm(g_ref[...], wd_ref[...], NT)

    @pl.when((i > 0) & (i < steps - 1))
    def _():
        both[...] += mm(r_ref[...], cat[part, :])
        hid[...] += mm(g_ref[...], wd_ref[...], NT)

    @pl.when(i == steps - 1)
    def _():
        for c in range(rows // chunk):
            at = slice(c * chunk, (c + 1) * chunk)
            total = both[at, :] + mm(r_ref[at, :], cat[part, :])
            d = hid[at, :] + mm(g_ref[at, :], wd_ref[...], NT)
            g, u = total[:, :hidden], total[:, hidden:]
            sig = jax.nn.sigmoid(g)
            silu = g * sig
            h_ref[at, :] = (silu * u).astype(BF16)
            a_ref[at, :hidden] = (d * u * (sig * (1.0 + g * (1.0 - sig)))).astype(BF16)
            a_ref[at, hidden:] = (d * silu).astype(BF16)

    @pl.when(i >= steps)
    def _():
        ret_ref[...] = mm(a_ref[...], cat[part, :], NT).astype(BF16)


def weights_body(r_ref, g_ref, h_ref, a_ref, dg_ref, du_ref, dd_ref):
    width = r_ref.shape[1]
    hidden = h_ref.shape[1]
    chunk = 256

    @pl.loop(0, width // chunk)
    def _(c):
        cols = pl.ds(pl.multiple_of(c * chunk, chunk), chunk)
        both = mm(r_ref[:, cols], a_ref[...], TN)
        dg_ref[cols, :] = both[:, :hidden].astype(BF16)
        du_ref[cols, :] = both[:, hidden:].astype(BF16)
        dd_ref[:, cols] = mm(h_ref[...], g_ref[:, cols], TN).astype(BF16)


def combine_body(head, scaling, mt_ref, ret_ref, og_ref, q_ref, ag_ref, lg_ref):
    width = og_ref.shape[1]
    rows = ret_ref.shape[1]
    total = og_ref[...].astype(F32)
    for p in range(2):
        both = (ret_ref[2 * p].astype(F32) + ret_ref[2 * p + 1].astype(F32)).astype(BF16)
        total = total + mm(mt_ref[:, p * rows : (p + 1) * rows], both)
    grad = total.astype(BF16)
    ag_ref[...] = grad
    for h in range(width // head):
        cols = slice(h * head, (h + 1) * head)
        lg_ref[cols, :] = (scaling * mm(q_ref[:, cols], grad[:, cols], TN)).astype(BF16)


def back_query_body(head, scaling, mk_ref, v_ref, ag_ref, s_ref, gq_ref):
    length, width = mk_ref.shape
    t = lax.broadcasted_iota(jnp.int32, (length, length), 0)
    s = lax.broadcasted_iota(jnp.int32, (length, length), 1)
    for h in range(width // head):
        cols = slice(h * head, (h + 1) * head)
        ag = ag_ref[:, cols]
        back = jnp.where(t >= s, mm(ag, v_ref[:, cols], NT), 0.0).astype(BF16)
        total = mm(back, mk_ref[:, cols]) + mm(ag, s_ref[cols, :], NT)
        gq_ref[:, cols] = (scaling * total).astype(BF16)


def back_body(head, scaling, q_ref, mk_ref, v_ref, ag_ref, gk_ref, gv_ref):
    length, width = q_ref.shape
    s = lax.broadcasted_iota(jnp.int32, (length, length), 0)
    t = lax.broadcasted_iota(jnp.int32, (length, length), 1)
    for h in range(width // head):
        cols = slice(h * head, (h + 1) * head)
        q, ag = q_ref[:, cols], ag_ref[:, cols]
        back = jnp.where(t >= s, mm(v_ref[:, cols], ag, NT), 0.0).astype(BF16)
        gk_ref[:, cols] = (scaling * mm(back, q)).astype(BF16)
        scores = jnp.where(t >= s, mm(mk_ref[:, cols], q, NT), 0.0).astype(BF16)
        gv_ref[:, cols] = (scaling * mm(scores, ag)).astype(BF16)


def final_body(head, mk_ref, v_ref, s_ref, g_ref, gki_ref, gvi_ref, gk_ref, gv_ref):
    width = mk_ref.shape[1]
    gate = spike_columns(s_ref[...], pl.program_id(0), width, head)
    for h in range(width // head):
        cols = slice(h * head, (h + 1) * head)
        state = g_ref[cols, :]
        gk = gki_ref[:, cols].astype(F32) + mm(v_ref[:, cols], state, NT)
        gk_ref[:, cols] = (gate[:, cols] * gk).astype(BF16)
        gv_ref[:, cols] = (gvi_ref[:, cols].astype(F32) + mm(mk_ref[:, cols], state)).astype(BF16)


def shape(*dims, dtype=BF16):
    return jax.ShapeDtypeStruct(dims, dtype)


def on_device(
    queries,
    key_vectors,
    value_vectors,
    spikes,
    routes,
    route_probs,
    gate_weight,
    up_weight,
    down_weight,
    out_grad,
):
    length, width = queries.shape
    heads = spikes.shape[1]
    head = width // heads
    tokens, model = out_grad.shape
    top = routes.shape[1]
    ctx = lax.axis_size("ctx")
    exp = lax.axis_size("exp")
    devices = ctx * exp
    experts = devices // 2
    capacity = 2 * max(1, 3 * tokens * top // (4 * experts))
    scaling = 1.0 / math.sqrt(head * length * ctx)
    hidden = gate_weight.shape[2]
    slots = exp * capacity
    half_rows = ctx * slots
    rows = 2 * half_rows
    pair = 4 * head
    pairs = width // pair
    everywhere = ("exp", "ctx")

    def cols(n=1, m=1):
        return pl.BlockSpec((n, m), lambda i: (0, i))

    def whole(*dims):
        return pl.BlockSpec(dims, lambda i: (0,) * len(dims))

    tall = pl.BlockSpec((pair, head), lambda i: (i, 0))
    wide = cols(length, pair)
    seq = shape(length, width)
    unit = length * width * 2
    spikes_t = spikes.T

    def exchange(part, reverse, cover):
        pieces = part.reshape(ctx, heads * head // ctx, head)
        pieces = lax.all_to_all(pieces, "ctx", 0, 0, tiled=True)
        pieces, cover = lax.optimization_barrier((pieces, cover))
        pieces = call(
            functools.partial(sum_body, reverse), (1,),
            [whole(*pieces.shape)], whole(*pieces.shape), shape(*pieces.shape), 1e6, 1 << 19, 4,
        )(pieces)
        pieces = lax.all_to_all(pieces, "ctx", 0, 0, tiled=True)
        return pieces.reshape(heads * head, head), cover

    block_state, masked = call(
        functools.partial(state_body, head), (pairs,),
        [wide, wide, whole(heads, length)], [tall, wide],
        [shape(heads * head, head), seq], 2 * length * width * head, 3 * unit,
    )(key_vectors, value_vectors, spikes_t)
    mine = lax.axis_index("exp").reshape(1)
    smem = pl.BlockSpec(memory_space=pltpu.SMEM)
    piece = (tokens + 16, width)
    own_grad, block_state = lax.optimization_barrier((out_grad, block_state))
    pieces = call(
        functools.partial(cut_body, capacity, slots, half_rows), (1,),
        [smem, whole(tokens, model), whole(top, tokens), whole(top, tokens)],
        [whole(*piece)] * exp, [shape(*piece)] * exp, 1e6, 2 * unit,
    )(mine, own_grad, routes.T, route_probs.T)
    pieces = list(pieces)
    for i in sorted(range(1, exp), key=lambda i: -min(i, exp - i)):
        pieces[i] = lax.ppermute(pieces[i], "exp", [(j, (j + i) % exp) for j in range(exp)])
    states_in, _ = exchange(block_state, False, ())
    intra = call(
        functools.partial(intra_body, head), (pairs,), [wide] * 3, wide, seq,
        4 * length * length * width, 4 * unit,
    )(queries, masked, value_vectors)

    send_shape = shape(2, 2, half_rows, 2 * width)
    send_flops = 2 * rows * length * width
    send_bytes = 4 * rows * width + 2 * rows * length + 2 * unit
    grad_cols, select, buffer = call(
        functools.partial(prepare_body, exp), (pairs,), [smem] + [whole(*piece)] * exp,
        [
            whole(length, width), whole(rows, length),
            pl.BlockSpec((2, 2, half_rows, pair), lambda i: (0, 0, 0, i + pairs)),
        ],
        [seq, shape(rows, length), send_shape], send_flops, send_bytes,
        scratch_shapes=[pltpu.VMEM((rows, length), BF16)],
    )(mine, *pieces)
    buffer = call(
        functools.partial(rows_body, head, scaling), (pairs,),
        [whole(rows, length), wide, wide, tall, pl.BlockSpec(memory_space=pl.ANY)],
        pl.BlockSpec((2, 2, half_rows, pair), lambda i: (0, 0, 0, i)),
        send_shape, send_flops, send_bytes, 52, input_output_aliases={4: 0},
    )(select, queries, intra, states_in, buffer)
    got = lax.all_to_all(
        buffer.reshape(devices, slots, 2 * width), everywhere, 0, 0, tiled=True
    ).reshape(exp * half_rows, 2 * width)

    act = shape(half_rows, hidden)
    last = exp - 1
    block = half_rows * width * 2
    back_rows, hid, acts = call(
        functools.partial(expert_body, exp), (2 * exp,),
        [
            pl.BlockSpec((half_rows, width), lambda i: (jnp.minimum(i, last), 0)),
            pl.BlockSpec((half_rows, width), lambda i: (jnp.minimum(i, last), 1)),
            pl.BlockSpec((width, hidden), lambda i: (jnp.minimum(i, last), 0)),
            pl.BlockSpec((width, hidden), lambda i: (jnp.minimum(i, last), 0)),
            pl.BlockSpec((hidden, width), lambda i: (0, jnp.minimum(i, last))),
        ],
        [
            pl.BlockSpec((half_rows, width), lambda i: (jnp.maximum(i - exp, 0), 0)),
            whole(half_rows, hidden),
            whole(half_rows, 2 * hidden),
        ],
        [shape(exp * half_rows, width), act, shape(half_rows, 2 * hidden)],
        10 * half_rows * model * hidden, 12 * block + 10 * model * hidden,
        scratch_shapes=[
            pltpu.VMEM((half_rows, 2 * hidden), F32), pltpu.VMEM((half_rows, hidden), F32),
            pltpu.VMEM((model, 2 * hidden), BF16),
        ],
    )(got, got, gate_weight[0], up_weight[0], down_weight[0])
    returned = lax.all_to_all(
        back_rows.reshape(devices, slots, width), everywhere, 0, 0, tiled=True
    ).reshape(exp, half_rows, width)
    grad_gate, grad_up, grad_down = call(
        weights_body, (exp,),
        [
            pl.BlockSpec((half_rows, width), lambda i: (i, 0)),
            pl.BlockSpec((half_rows, width), lambda i: (i, 1)),
            whole(half_rows, hidden),
            whole(half_rows, 2 * hidden),
        ],
        [
            pl.BlockSpec((width, hidden), lambda i: (i, 0)),
            pl.BlockSpec((width, hidden), lambda i: (i, 0)),
            pl.BlockSpec((hidden, width), lambda i: (0, i)),
        ],
        [shape(model, hidden), shape(model, hidden), shape(hidden, model)],
        6 * half_rows * model * hidden, 8 * block + 6 * model * hidden,
    )(got, got, hid, acts)

    far_pieces, acts = lax.optimization_barrier((tuple(pieces), acts))
    select_t = call(
        functools.partial(select_t_body, exp), (1,), [smem] + [whole(*piece)] * exp,
        whole(length, rows), shape(length, rows), 1e6, 2 * rows * length + unit,
    )(mine, *far_pieces)
    returned, select_t, grad_gate, grad_up, grad_down = lax.optimization_barrier(
        (returned, select_t, grad_gate, grad_up, grad_down)
    )

    att_grad, local_grad = call(
        functools.partial(combine_body, head, scaling), (pairs,),
        [whole(length, rows), pl.BlockSpec((exp, half_rows, pair), lambda i: (0, 0, i)), wide, wide],
        [wide, tall], [seq, shape(heads * head, head)],
        2 * rows * length * width, 2 * rows * length + 4 * block + 3 * unit,
    )(select_t, returned, grad_cols, queries)
    parts = call(
        functools.partial(back_body, head, scaling), (pairs,), [wide] * 4, [wide] * 2,
        [seq, seq], 8 * length * length * width, 6 * unit,
    )(queries, masked, value_vectors, att_grad)
    grad_states, (keys_part, values_part) = exchange(local_grad, True, tuple(parts))
    grad_queries = call(
        functools.partial(back_query_body, head, scaling), (pairs,), [wide] * 3 + [tall], wide, seq,
        4 * length * length * width, 4 * unit,
    )(masked, value_vectors, att_grad, states_in)
    grad_keys, grad_values = call(
        functools.partial(final_body, head), (pairs,),
        [wide, wide, whole(heads, length), tall, wide, wide], [wide] * 2, [seq, seq],
        4 * length * width * head, 6 * unit, 52,
    )(masked, value_vectors, spikes_t, grad_states, keys_part, values_part)
    return grad_queries, grad_keys, grad_values, grad_gate[None], grad_up[None], grad_down[None]


def solution(mesh):
    by_head = P("ctx", "exp")
    by_device = P(("ctx", "exp"), None)
    by_half = P(("ctx", "exp"), None, None)
    return jax.shard_map(
        on_device,
        mesh=mesh,
        in_specs=(by_head,) * 4 + (by_device,) * 2 + (by_half,) * 3 + (by_device,),
        out_specs=(by_head,) * 3 + (by_half,) * 3,
        check_vma=False,
    )
```
